32 devices in a mesh: rep: 2 (over y), seq: 4 (over z), head: 2 (over x), sub: 2 (over core).
Axes of the slice: x: 2, y: 2, z: 4, core: 2. Of those that a mesh axis runs over, the one named last changes fastest.
Arguments:
- key_cache: float32 [8, 32768, 128], P('head', ('rep', 'seq')), parts along dimension 1, may hold values from -40 to 40
- value_cache: bfloat16 [8, 32768, 128], P('head', ('rep', 'seq')), parts along dimension 1, may hold values from -6 to 6
- centroids: float32 [8, 1024, 128], P('head', ('rep', 'sub')), parts along dimension 1, may hold values from -8 to 8
- inv_temp: float32 [8], P('head'), may hold values from 0.015625 to 0.078125
- page_owner: int32 [8, 256, 1], P('head', ('rep', 'seq')), parts along dimension 1, may hold values from 0 to 3; in each aligned block of 32 rows (0 to 31, 32 to 63, ..., all dimensions but the last counted through in order) at most 12 rows name the same one
Outputs:
- clusters: float32 [8, 1024, 128], P('head', ('rep', 'sub')), parts along dimension 1
- moved_keys: bfloat16 [8, 384, 128, 128], P('head', ('rep', 'seq')), parts along dimension 1
- moved_values: bfloat16 [8, 384, 128, 128], P('head', ('rep', 'seq')), parts along dimension 1
- page_ids: int32 [8, 384], P('head', ('rep', 'seq')), parts along dimension 1
The draws below stay inside these ranges and needn't reach their ends.
There are 2 independent parts, one for each index of `rep`. The reference program is written for one: setup_inputs(seed, part) draws one part's arguments, and reference() takes and returns one part's arrays. A program takes and returns all parts, laid end to end along the dimension named above; an argument that names none is the same for every part. Nothing has to cross between parts.
Inputs may be any that keep to these rules, and one draw needn't show every extreme that they name: `page_owner`: among the 32 pages of one head on one index of seq (an aligned block), no owner is named by more than 12 pages, a bound that some block reaches.
All inputs are finite; a program needn't handle non-finite values.
Results may differ from the reference program's by a relative error of at most 0.0075.
Values may be sent and summed in bfloat16 or wider, within the bound.
No kernel may reach another device: no remote copies, remote signals or barrier semaphores. Data moves between devices by JAX's collectives and lax.ppermute only.
A program may use at most 128 MiB of HBM per device.

```python
import math
import jax
import jax.numpy as jnp
import numpy as np
from jax import lax

HEADS = 8
DH = 128
CENT = 512
ITERS = 3
PAGE = 128
TOKENS = 16384
PAGE_DEV = 32
PAGES = 128
CAP = 12
SLOTS = 192
N_SEQ = 4


def cluster_centers(key):
    base_draw = jax.random.normal(jax.random.fold_in(key, 11), (HEADS, CENT, DH), jnp.float32)
    return 0.6 * base_draw + 0.8 * jnp.roll(base_draw, 1, axis=1)


def draw_key_cache(key, part):
    centers = cluster_centers(key)
    positions = jnp.arange(TOKENS, dtype=jnp.int32)
    jitter = jax.random.randint(jax.random.fold_in(key, 12), (HEADS, TOKENS), 0, 4)
    labels = (positions[None, :] * CENT // TOKENS + jitter) % CENT
    located = jax.vmap(lambda table_rows, label_rows: jnp.take(table_rows, label_rows, axis=0))(centers, labels)
    noise = 0.5 * jax.random.normal(jax.random.fold_in(key, 13), (HEADS, TOKENS, DH), jnp.float32)
    marked = (positions % 509 == 0)[None, :, None]
    amplitude = (30 + 5 * (positions // 509 % 3)).astype(jnp.float32)[None, :, None]
    loud = amplitude * jnp.sign(located)
    drawn = jnp.where(marked, loud, located + noise)
    return jnp.clip(drawn, -40.0, 40.0)


def draw_centroids(key, part):
    centers = cluster_centers(key)
    noise = jax.random.normal(jax.random.fold_in(key, 15), (HEADS, CENT, DH), jnp.float32)
    drawn = centers + 0.3 * noise
    return jnp.clip(drawn, -8.0, 8.0)


def steps_of(stream_key, dims, shards, low, top_value):
    level, own = 1.0, jax.random.fold_in(stream_key, 6)
    for axis_at, parts in shards:
        draws = jnp.exp(jax.random.uniform(jax.random.fold_in(own, axis_at), (parts,), jnp.float32, low / len(shards), top_value / len(shards)))
        level = level * jnp.repeat(draws, dims[axis_at] // parts).reshape([-1 if axis == axis_at else 1 for axis in range(len(dims))])
    return level


def routed_block(stream_key, own, number, rows, count, top, reach, lean):
    sequence = jax.random.permutation(stream_key, count)
    crowded, usual = portions_of(count, rows * top, reach, lean, True), portions_of(count, rows * top, reach, lean, False)
    places = jnp.arange(count)

    def named(tallies, rotation):
        used = int((tallies > 0).sum())
        fixed = max(1, used // 4)
        passed = fixed + (places - fixed + rotation * (used - fixed)) % max(1, count - fixed)
        return jnp.zeros((count,), jnp.int32).at[sequence[jnp.where(places < fixed, places, passed)]].set(jnp.asarray(tallies, jnp.int32))

    tallies = jnp.where(number % 4 == 0, named(crowded, number // 4), named(usual, number - number // 4 - 1))
    mixed = jax.random.permutation(jax.random.fold_in(own, 3), count)
    donor, sink = mixed[0:count // 2 * 2:2], mixed[1:count // 2 * 2:2]
    margin = jnp.minimum(tallies[donor] - 1, reach - tallies[sink]) // 2
    margin = jnp.where((donor == sequence[0]) | (sink == sequence[0]) | (tallies[sink] == 0), 0, jnp.maximum(margin, 0))
    passed = jax.random.randint(jax.random.fold_in(own, 4), (count // 2,), 0, 1 << 20) % (margin + 1)
    tallies = tallies.at[donor].add(-passed).at[sink].add(passed)
    members = jnp.searchsorted(jnp.cumsum(tallies), jnp.arange(rows * top), side="right").astype(jnp.int32)
    listing = members.reshape(top, rows).T
    listing = listing[jax.random.permutation(jax.random.fold_in(own, 1), rows)]
    rotation = jax.random.randint(jax.random.fold_in(own, 2), (rows, 1), 0, top)
    return jnp.take_along_axis(listing, (jnp.arange(top)[None, :] + rotation) % top, axis=1)


def portions_of(count, total, limit, lean, full):
    portions = [(1 << 20) // math.isqrt(standing ** lean) + 1 for standing in range(1, count + 1)]
    largest = limit if full else min(limit, max(-(-total // count), total * portions[0] // sum(portions)))
    least = 1 if total - largest >= count - 1 else 0
    holding, rest = [largest] + [least] * (count - 1), total - largest - least * (count - 1)
    while rest > 0:
        candidates = [i for i in range(1, count) if holding[i] < largest] or [i for i in range(1, count) if holding[i] < limit]
        pool, remaining = sum([portions[i] for i in candidates]), rest
        for i in candidates:
            more = min(limit - holding[i], max(1, remaining * portions[i] // pool), rest)
            holding[i] = holding[i] + more
            rest = rest - more
    return np.array(holding)


def normal_values(own_key, extent, deviation, limit, shards=(), kind=jnp.bfloat16):
    result = deviation * jax.random.normal(own_key, extent, jnp.float32)
    if shards:
        result = result * steps_of(own_key, extent, shards, -0.22, 0.18)
    return jnp.clip(result, -limit, limit).astype(kind)


def setup_inputs(seed: int = 0, part: int = 0) -> dict:
    seeds = jax.random.split(jax.random.key(seed), 6)
    part_keys = jax.random.split(jax.random.fold_in(seeds[5], part), 6)
    key_cache = draw_key_cache(jax.random.fold_in(jax.random.fold_in(seeds[5], part), 71), part)
    value_cache = normal_values(part_keys[1], (HEADS, TOKENS, DH), 1.0, 6.0, ((0, 2), (1, 4)))
    centroids = draw_centroids(jax.random.fold_in(jax.random.fold_in(seeds[5], part), 71), part)
    inv_temp = jnp.clip(jnp.exp(math.log(0.078125) - 1.609438 * jax.random.uniform(seeds[3], (HEADS,), jnp.float32) ** steps_of(seeds[3], (HEADS,), ((0, 2),), -0.2, 0.2)), 0.015625, 0.078125)
    page_owner_keys = jax.random.split(jax.random.fold_in(part_keys[4], 1), HEADS * PAGES // PAGE_DEV)
    page_owner_turns = jax.random.permutation(jax.random.fold_in(part_keys[4], 3), HEADS * PAGES // PAGE_DEV)
    page_owner = jax.vmap(lambda own, number: routed_block(jax.random.fold_in(part_keys[4], 2), own, number, PAGE_DEV, N_SEQ, 1, CAP, 2))(page_owner_keys, page_owner_turns).reshape((HEADS, PAGES, 1))
    return {"key_cache": key_cache, "value_cache": value_cache, "centroids": centroids, "inv_temp": inv_temp, "page_owner": page_owner}


prior_count = 8.0


def page_slots(page_owner, owner_count, capacity):
    owner_ids = jnp.arange(owner_count, dtype=jnp.int32)
    owner_hits = (page_owner[:, None, :] == owner_ids[None, :, None]).astype(jnp.int32)
    before = jnp.cumsum(owner_hits, axis=2) - owner_hits
    slot_ids = jnp.arange(capacity, dtype=jnp.int32)
    matched = (owner_hits[:, :, None, :] == 1) & (before[:, :, None, :] == slot_ids[None, None, :, None])
    page_index = jnp.arange(page_owner.shape[1], dtype=jnp.int32)
    source = jnp.sum(jnp.where(matched, page_index[None, None, None, :], 0), axis=3).astype(jnp.int32)
    filled = jnp.any(matched, axis=3)
    head_count = page_owner.shape[0]
    return source.reshape(head_count, owner_count * capacity), filled.reshape(head_count, owner_count * capacity)


def head_sweep(operands):
    keys_head, cent_head, head_rate = operands
    low_table = cent_head.astype(jnp.bfloat16)
    half_norm = 0.5 * jnp.sum(cent_head * cent_head, axis=1)
    scores = jnp.dot(keys_head, low_table.T, preferred_element_type=jnp.float32)
    logits = head_rate * (scores - half_norm[None, :])
    highest = jnp.max(logits, axis=1, keepdims=True)
    spread = jnp.exp(logits - highest)
    weights = (spread / jnp.sum(spread, axis=1, keepdims=True)).astype(jnp.bfloat16)
    key_sums = jnp.dot(weights.T, keys_head, preferred_element_type=jnp.float32)
    resp_mass = jnp.sum(weights.astype(jnp.float32), axis=0)
    return (key_sums + prior_count * cent_head) / (resp_mass[:, None] + prior_count)


def pick_pages(page_rows, global_index, filled):
    picked = jax.vmap(lambda head_block, row_index: jnp.take(head_block, row_index, axis=0))(page_rows, global_index)
    return jnp.where(filled[:, :, None, None], picked, jnp.zeros((), page_rows.dtype))


def reference(key_cache, value_cache, centroids, inv_temp, page_owner):
    keys_low = key_cache.astype(jnp.bfloat16)
    cent_table = centroids
    for iteration in range(ITERS):
        cent_table = lax.map(head_sweep, (keys_low, cent_table, inv_temp))
    clusters = cent_table

    owner_grid = page_owner[:, :, 0].reshape(HEADS, N_SEQ, PAGE_DEV)
    source, filled = jax.vmap(lambda owner_rows: page_slots(owner_rows, N_SEQ, CAP), in_axes=1, out_axes=1)(owner_grid)
    source = source.reshape(HEADS, N_SEQ, N_SEQ, CAP)
    filled = filled.reshape(HEADS, N_SEQ, N_SEQ, CAP)
    source_base = (PAGE_DEV * jnp.arange(N_SEQ, dtype=jnp.int32))[None, :, None, None]
    global_index = (source + source_base).astype(jnp.int32)
    global_index = jnp.transpose(global_index, (0, 2, 1, 3)).reshape(HEADS, SLOTS)
    filled = jnp.transpose(filled, (0, 2, 1, 3)).reshape(HEADS, SLOTS)
    page_ids = jnp.where(filled, global_index, -1).astype(jnp.int32)
    moved_keys = pick_pages(keys_low.reshape(HEADS, PAGES, PAGE, DH), global_index, filled)
    moved_values = pick_pages(value_cache.reshape(HEADS, PAGES, PAGE, DH), global_index, filled)
    return (clusters, moved_keys, moved_values, page_ids)
```

```python
import functools

import jax
import jax.numpy as jnp
from jax import lax
from jax.experimental import pallas as pl
from jax.experimental.pallas import tpu as pltpu
from jax.sharding import PartitionSpec as P

ITERS = 3
PAGE = 128
PRIOR = 8.0
TAIL = 16
LOG2E = 1.4426950408889634


def chunk_plan(ranks, heads, capacity):
    plan = []
    for head in range(heads):
        for shift in range(1, ranks):
            crossing = min(shift, ranks - shift)
            pieces = crossing if capacity % crossing == 0 else 1
            for piece in range(pieces):
                plan.append((shift, head, piece * (capacity // pieces), capacity // pieces))
    return plan


def fill_table(owner_ref, table_ref, count_ref, head, ranks, capacity, pages):
    def clear(slot, carry):
        table_ref[slot] = pages
        return carry

    lax.fori_loop(0, ranks * capacity, clear, 0)
    for rank in range(ranks):
        count_ref[rank] = 0

    def put(page, carry):
        owner = owner_ref[head, page]
        place = count_ref[owner]
        table_ref[owner * capacity + place] = page
        count_ref[owner] = place + 1
        return carry

    lax.fori_loop(0, pages, put, 0)


def scatter_kernel(plan, ranks, capacity, pages, with_cast, owner_ref, cache_ref, *refs):
    chunk_refs, refs = refs[: len(plan)], refs[len(plan) :]
    if with_cast:
        low_ref, local_ref, wide_ref, page_ref, table_ref, count_ref, in_sem, chunk_sem, local_sem, low_sem = refs
    else:
        local_ref, page_ref, table_ref, count_ref, in_sem, chunk_sem, local_sem = refs
    heads = cache_ref.shape[0]
    me = lax.axis_index("seq")
    core = lax.axis_index("sub")
    share = heads // lax.axis_size("sub")
    order = [(core * share + i) for i in range(share)]
    order += [lax.rem(core * share + i, heads) for i in range(share, heads)]
    into = wide_ref if with_cast else page_ref
    loads = []
    for i, head in enumerate(order):
        target = into.at[i] if with_cast else into.at[i, pl.ds(0, pages)]
        load = pltpu.make_async_copy(cache_ref.at[head], target, in_sem.at[i])
        load.start()
        loads.append(load)
    for i in range(heads):
        page_ref[i, pages] = jnp.zeros(page_ref.shape[2:], page_ref.dtype)
    for i, head in enumerate(order):
        fill_table(owner_ref, table_ref, count_ref, head, ranks, capacity, pages)
        loads[i].wait()
        if with_cast:

            def cast(page, carry, i=i):
                page_ref[i, page] = wide_ref[i, page].astype(page_ref.dtype)
                return carry

            lax.fori_loop(0, pages, cast, 0, unroll=2)
            if i < share:
                pltpu.make_async_copy(page_ref.at[i, pl.ds(0, pages)], low_ref.at[i], low_sem.at[i]).start()
        for j, (shift, chunk_head, first, size) in enumerate(plan):
            if chunk_head != i:
                continue
            base = lax.rem(me + shift, ranks) * capacity + first

            def send(slot, carry, i=i, j=j, base=base):
                page = table_ref[base + slot]
                pltpu.make_async_copy(page_ref.at[i, page], chunk_refs[j].at[slot], chunk_sem.at[j]).start()
                return carry

            lax.fori_loop(0, size, send, 0)

        def keep(slot, carry, i=i, head=head):
            place = me * capacity + slot
            page = table_ref[place]
            pltpu.make_async_copy(page_ref.at[i, page], local_ref.at[head, place], local_sem).start()
            return carry

        lax.fori_loop(0, capacity, keep, 0)
    for j in range(len(plan)):
        pltpu.make_async_copy(chunk_refs[j], chunk_refs[j], chunk_sem.at[j]).wait()
    if with_cast:
        for i in range(share):
            pltpu.make_async_copy(low_ref.at[i], low_ref.at[i], low_sem.at[i]).wait()
    kept = local_ref.at[:, pl.ds(0, capacity)]
    pltpu.make_async_copy(kept, kept, local_sem).wait()


def scatter_pages(owner, cache, plan, ranks, capacity, with_cast):
    heads, tokens, width = cache.shape
    pages = tokens // PAGE
    share = heads // lax.axis_size("sub")
    page_shape = (PAGE, width)
    low = jnp.bfloat16
    anywhere = pl.BlockSpec(memory_space=pl.ANY)
    out_shape = [jax.ShapeDtypeStruct((size,) + page_shape, low) for _, _, _, size in plan]
    if with_cast:
        out_shape.append(jax.ShapeDtypeStruct((share, pages) + page_shape, low))
    out_shape.append(jax.ShapeDtypeStruct((heads, ranks * capacity) + page_shape, low))
    scratch = []
    if with_cast:
        scratch.append(pltpu.VMEM((heads, pages) + page_shape, cache.dtype))
    scratch += [
        pltpu.VMEM((heads, pages + 1) + page_shape, low),
        pltpu.SMEM((ranks * capacity,), jnp.int32),
        pltpu.SMEM((ranks,), jnp.int32),
        pltpu.SemaphoreType.DMA((heads,)),
        pltpu.SemaphoreType.DMA((len(plan),)),
        pltpu.SemaphoreType.DMA,
    ]
    if with_cast:
        scratch.append(pltpu.SemaphoreType.DMA((share,)))
    return pl.pallas_call(
        functools.partial(scatter_kernel, plan, ranks, capacity, pages, with_cast),
        out_shape=out_shape,
        in_specs=[pl.BlockSpec(memory_space=pltpu.SMEM), anywhere],
        out_specs=[anywhere] * len(out_shape),
        scratch_shapes=scratch,
        name="scatter_keys" if with_cast else "scatter_values",
        cost_estimate=pl.CostEstimate(flops=0, bytes_accessed=16 << 20, transcendentals=0),
    )(owner, cache.reshape((heads, pages) + page_shape))


def tail_rows(first, second, dtype):
    rows = lax.broadcasted_iota(jnp.int32, (TAIL, PAGE), 0)
    return jnp.where(rows == 0, first, jnp.where(rows == 1, second, 0.0)).astype(dtype)


def split_mass(mass):
    high = mass.astype(jnp.bfloat16).astype(jnp.float32)
    rows = lax.broadcasted_iota(jnp.int32, mass.shape, 0)
    blocks = mass.shape[0] // 2
    held = jnp.where(rows < blocks // 4, high, 0.0)
    rest = jnp.where(rows < blocks // 4, mass - high, 0.0)
    return (held + pltpu.roll(rest, blocks // 4, 0)).astype(jnp.bfloat16)


def join_mass(tail):
    wide = tail.astype(jnp.float32)
    return wide + pltpu.roll(wide, TAIL - TAIL // 8, 0)


def sweep_kernel(tile, temp_ref, keys_ref, own_ref, other_ref, keep_ref, send_ref, sums_ref, table_ref):
    half, width = own_ref.shape[1:]
    core = lax.axis_index("sub")
    rate = temp_ref[core * pl.num_programs(0) + pl.program_id(0)] * LOG2E
    lane = lax.broadcasted_iota(jnp.int32, (half, width), 1)
    for part, ref in ((0, own_ref), (1, other_ref)):
        table = ref[0]
        norm = -0.5 * jnp.sum(table * table, axis=1, keepdims=True)
        high = norm.astype(jnp.bfloat16).astype(jnp.float32)
        mid = (norm - high).astype(jnp.bfloat16).astype(jnp.float32)
        low = norm - high - mid
        extra = jnp.where(lane == 0, high, jnp.where(lane == 1, mid, jnp.where(lane == 2, low, 0.0)))
        rows = pl.ds(part * half, half)
        table_ref[rows, 0:width] = table.astype(jnp.bfloat16)
        table_ref[rows, width : 2 * width] = extra.astype(jnp.bfloat16)
    sums_ref[...] = jnp.zeros_like(sums_ref)

    def step(at, carry):
        keys = keys_ref[0, pl.ds(pl.multiple_of(at * tile, tile), tile), :]
        wide = jnp.concatenate([keys, jnp.ones_like(keys)], axis=1)
        scores = lax.dot_general(
            table_ref[...], wide, (((1,), (1,)), ((), ())), preferred_element_type=jnp.float32
        )
        highest = jnp.max(scores, axis=0, keepdims=True)
        spread = jnp.exp2((scores - highest) * rate)
        total = jnp.sum(spread, axis=0, keepdims=True)
        weights = (spread * (1.0 / total)).astype(jnp.bfloat16)
        sums_ref[...] += jnp.dot(weights, wide, preferred_element_type=jnp.float32)
        return carry

    lax.fori_loop(0, keys_ref.shape[1] // tile, step, 0, unroll=2)
    masses = []
    for block in range(2 * half // width):
        masses.append(jnp.transpose(sums_ref[pl.ds(block * width, width), width : 2 * width])[0:TAIL])
    keep_ref[0, 0:half] = sums_ref[0:half, 0:width]
    keep_ref[0, half : half + TAIL] = tail_rows(masses[0], masses[1], jnp.float32)
    send_ref[0, 0:half] = sums_ref[half : 2 * half, 0:width].astype(jnp.bfloat16)
    send_ref[0, half : half + TAIL] = split_mass(tail_rows(masses[2], masses[3], jnp.float32))


def sweep(temp, keys, own, other, tile):
    heads, tokens, width = keys.shape
    half = own.shape[1]
    table_spec = pl.BlockSpec((1, half, width), lambda h: (h, 0, 0))
    load_spec = pl.BlockSpec((1, half + TAIL, width), lambda h: (h, 0, 0))
    return pl.pallas_call(
        functools.partial(sweep_kernel, tile),
        grid=(heads,),
        in_specs=[
            pl.BlockSpec(memory_space=pltpu.SMEM),
            pl.BlockSpec((1, tokens, width), lambda h: (h, 0, 0)),
            table_spec,
            table_spec,
        ],
        out_specs=[load_spec, load_spec],
        out_shape=[
            jax.ShapeDtypeStruct((heads, half + TAIL, width), jnp.float32),
            jax.ShapeDtypeStruct((heads, half + TAIL, width), jnp.bfloat16),
        ],
        scratch_shapes=[
            pltpu.VMEM((2 * half, 2 * width), jnp.float32),
            pltpu.VMEM((2 * half, 2 * width), jnp.bfloat16),
        ],
        name="sweep",
        cost_estimate=pl.CostEstimate(
            flops=8 * heads * tokens * half * width, bytes_accessed=2 * heads * tokens * width, transcendentals=2 * heads * tokens * half
        ),
    )(temp, keys, own, other)


def join_kernel(left_ref, right_ref, out_ref):
    half = left_ref.shape[1] - TAIL
    for head in range(left_ref.shape[0]):
        body = left_ref[head, 0:half].astype(jnp.float32) + right_ref[head, 0:half].astype(jnp.float32)
        out_ref[head, 0:half] = body.astype(jnp.bfloat16)
        if left_ref.dtype == jnp.float32:
            mass = left_ref[head, half : half + TAIL]
        else:
            mass = join_mass(left_ref[head, half : half + TAIL])
        mass = mass + join_mass(right_ref[head, half : half + TAIL])
        out_ref[head, half : half + TAIL] = split_mass(mass)


def join(left, right):
    return pl.pallas_call(
        join_kernel,
        out_shape=jax.ShapeDtypeStruct(left.shape, jnp.bfloat16),
        name="join",
    )(left, right)


def renew_kernel(left_ref, right_ref, table_ref, out_ref):
    half, width = table_ref.shape[1:]
    for head in range(left_ref.shape[0]):
        mass = join_mass(left_ref[head, half : half + TAIL]) + join_mass(right_ref[head, half : half + TAIL])
        for block in range(half // width):
            rows = slice(block * width, (block + 1) * width)
            spread = jnp.transpose(jnp.broadcast_to(mass[block : block + 1], (width, width)))
            body = left_ref[head, rows].astype(jnp.float32) + right_ref[head, rows].astype(jnp.float32)
            out_ref[head, rows] = (body + PRIOR * table_ref[head, rows]) / (spread + PRIOR)


def renew(left, right, table):
    return pl.pallas_call(
        renew_kernel,
        out_shape=jax.ShapeDtypeStruct(table.shape, table.dtype),
        name="renew",
    )(left, right, table)


def tied(value, *others):
    return lax.optimization_barrier((value,) + others)


def on_device(key_cache, value_cache, centroids, inv_temp, page_owner):
    heads, tokens, width = key_cache.shape
    pages = tokens // PAGE
    ranks = lax.axis_size("seq")
    cores = lax.axis_size("sub")
    me, core = lax.axis_index("seq"), lax.axis_index("sub")
    share = heads // cores
    capacity = max(2, (3 * pages + 2 * ranks - 1) // (2 * ranks))
    owner = page_owner[:, :, 0]
    swap = [(0, 1), (1, 0)]
    ring = lambda shift: [(i, (i + shift) % ranks) for i in range(ranks)]
    facing = lambda bit: [(i, i ^ bit) for i in range(ranks)]

    owners = [owner] + [lax.ppermute(owner, "seq", ring(shift)) for shift in range(1, ranks)]

    mine = lax.dynamic_slice_in_dim(centroids, core * share, share, 0)
    theirs = lax.dynamic_slice_in_dim(centroids, (1 - core) * share, share, 0)
    got = lax.ppermute(theirs, "sub", swap)
    straight = lax.rem(me, 2) == core
    own = jnp.where(straight, mine, got)
    other = jnp.where(straight, got, mine)

    plan = chunk_plan(ranks, share, capacity)
    *value_chunks, moved_values = scatter_pages(owner, value_cache, plan, ranks, capacity, False)
    *key_chunks, keys_low, moved_keys = scatter_pages(owner, key_cache, plan, ranks, capacity, True)
    keys_low = keys_low.reshape(share, tokens, width)

    waiting = [(0, spec, chunk) for spec, chunk in zip(plan, value_chunks)]
    waiting += [(1, spec, chunk) for spec, chunk in zip(plan, key_chunks)]
    moved = [moved_values, moved_keys]
    arrived = []

    def issue(count, after=None):
        for _ in range(count):
            if not waiting:
                return
            which, spec, chunk = waiting.pop(0)
            if after is not None:
                chunk, _ = tied(chunk, after)
            arrived.append((which, spec, lax.ppermute(chunk, "seq", ring(spec[0]))))

    stages = ITERS * (1 + ranks.bit_length())
    per_stage = -(-len(waiting) // (stages + 1))
    issue(2)
    for iteration in range(ITERS):
        keep, send = sweep(inv_temp, keys_low, own, other, 512)
        got = lax.ppermute(send, "seq", facing(1))
        issue(per_stage, send)
        payload = join(keep, got)
        bit = 2
        while bit < ranks:
            got = lax.ppermute(payload, "seq", facing(bit))
            issue(per_stage, payload)
            bit *= 2
            if bit < ranks:
                payload = join(payload, got)
        own = renew(payload, got, own)
        other = lax.ppermute(own, "seq", facing(1))
        issue(per_stage, own)
    issue(len(waiting))

    for which, (shift, head, first, size), chunk in arrived:
        partner = lax.ppermute(chunk, "sub", swap)
        start = lax.rem(me - shift + ranks, ranks) * capacity + first
        place = lambda whole, part, at: lax.dynamic_update_slice(whole, part[None], (at, start, 0, 0))
        moved[which] = place(moved[which], chunk, core * share + head)
        moved[which] = place(moved[which], partner, (1 - core) * share + head)

    lower = jnp.where(lax.rem(me, 2) == 0, own, other)
    upper = jnp.where(lax.rem(me, 2) == 0, other, own)
    ours = jnp.where(core == 0, lower, upper)
    other_half = lax.ppermute(jnp.where(core == 0, upper, lower), "sub", swap)
    clusters = jnp.where(
        core == 0, jnp.concatenate([ours, other_half], axis=0), jnp.concatenate([other_half, ours], axis=0)
    )

    slot_ids = jnp.arange(capacity, dtype=jnp.int32)
    ids = jnp.full((heads, ranks * capacity), -1, jnp.int32)
    for shift in range(ranks):
        source = lax.rem(me - shift + ranks, ranks)
        hits = (owners[shift] == me).astype(jnp.int32)
        before = jnp.cumsum(hits, axis=1) - hits
        matched = (hits[:, None, :] == 1) & (before[:, None, :] == slot_ids[None, :, None])
        number = source * pages + jnp.arange(pages, dtype=jnp.int32)
        found = jnp.max(jnp.where(matched, number[None, None, :], -1), axis=2)
        ids = lax.dynamic_update_slice(ids, found, (0, source * capacity))
    return (clusters, moved[1], moved[0], ids)


def solution(mesh):
    return jax.shard_map(
        on_device,
        mesh=mesh,
        in_specs=(
            P("head", ("rep", "seq"), None),
            P("head", ("rep", "seq"), None),
            P("head", ("rep", "sub"), None),
            P("head"),
            P("head", ("rep", "seq"), None),
        ),
        out_specs=(
            P("head", ("rep", "sub"), None),
            P("head", ("rep", "seq"), None, None),
            P("head", ("rep", "seq"), None, None),
            P("head", ("rep", "seq")),
        ),
        check_vma=False,
    )
```

```python
import functools

import jax
import jax.numpy as jnp
from jax import lax
from jax.experimental import pallas as pl
from jax.experimental.pallas import tpu as pltpu
from jax.sharding import PartitionSpec as P

ITERS = 3
PAGE = 128
PRIOR = 8.0
TAIL = 16
LOG2E = 1.4426950408889634


def chunk_plan(ranks, heads, capacity):
    plan = []
    for head in range(heads):
        for shift in range(1, ranks):
            crossing = min(shift, ranks - shift)
            pieces = crossing if capacity % crossing == 0 else 1
            for piece in range(pieces):
                plan.append((shift, head, piece * (capacity // pieces), capacity // pieces))
    return plan


def fill_table(owner_ref, table_ref, count_ref, head, ranks, capacity, pages):
    def clear(slot, carry):
        table_ref[slot] = pages
        return carry

    lax.fori_loop(0, ranks * capacity, clear, 0)
    for rank in range(ranks):
        count_ref[rank] = 0

    def put(page, carry):
        owner = owner_ref[head, page]
        place = count_ref[owner]
        table_ref[owner * capacity + place] = page
        count_ref[owner] = place + 1
        return carry

    lax.fori_loop(0, pages, put, 0)


def scatter_kernel(plan, ranks, capacity, pages, with_cast, owner_ref, cache_ref, *refs):
    chunk_refs, refs = refs[: len(plan)], refs[len(plan) :]
    if with_cast:
        low_ref, local_ref, wide_ref, page_ref, table_ref, count_ref, in_sem, chunk_sem, local_sem, low_sem = refs
    else:
        local_ref, page_ref, table_ref, count_ref, in_sem, chunk_sem, local_sem = refs
    heads = cache_ref.shape[0]
    me = lax.axis_index("seq")
    core = lax.axis_index("sub")
    share = heads // lax.axis_size("sub")
    order = [(core * share + i) for i in range(share)]
    order += [lax.rem(core * share + i, heads) for i in range(share, heads)]
    into = wide_ref if with_cast else page_ref
    loads = []
    for i, head in enumerate(order):
        target = into.at[i] if with_cast else into.at[i, pl.ds(0, pages)]
        load = pltpu.make_async_copy(cache_ref.at[head], target, in_sem.at[i])
        load.start()
        loads.append(load)
    for i in range(heads):
        page_ref[i, pages] = jnp.zeros(page_ref.shape[2:], page_ref.dtype)
    for i, head in enumerate(order):
        fill_table(owner_ref, table_ref, count_ref, head, ranks, capacity, pages)
        loads[i].wait()
        if with_cast:

            def cast(page, carry, i=i):
                page_ref[i, page] = wide_ref[i, page].astype(page_ref.dtype)
                return carry

            lax.fori_loop(0, pages, cast, 0, unroll=2)
            if i < share:
                pltpu.make_async_copy(page_ref.at[i, pl.ds(0, pages)], low_ref.at[i], low_sem.at[i]).start()
        for j, (shift, chunk_head, first, size) in enumerate(plan):
            if chunk_head != i:
                continue
            base = lax.rem(me + shift, ranks) * capacity + first

            def send(slot, carry, i=i, j=j, base=base):
                page = table_ref[base + slot]
                pltpu.make_async_copy(page_ref.at[i, page], chunk_refs[j].at[slot], chunk_sem.at[j]).start()
                return carry

            lax.fori_loop(0, size, send, 0)

        def keep(slot, carry, i=i, head=head):
            place = me * capacity + slot
            page = table_ref[place]
            pltpu.make_async_copy(page_ref.at[i, page], local_ref.at[head, place], local_sem).start()
            return carry

        lax.fori_loop(0, capacity, keep, 0)
    for j in range(len(plan)):
        pltpu.make_async_copy(chunk_refs[j], chunk_refs[j], chunk_sem.at[j]).wait()
    if with_cast:
        for i in range(share):
            pltpu.make_async_copy(low_ref.at[i], low_ref.at[i], low_sem.at[i]).wait()
    kept = local_ref.at[:, pl.ds(0, capacity)]
    pltpu.make_async_copy(kept, kept, local_sem).wait()


def scatter_pages(owner, cache, plan, ranks, capacity, with_cast):
    heads, tokens, width = cache.shape
    pages = tokens // PAGE
    share = heads // lax.axis_size("sub")
    page_shape = (PAGE, width)
    low = jnp.bfloat16
    anywhere = pl.BlockSpec(memory_space=pl.ANY)
    out_shape = [jax.ShapeDtypeStruct((size,) + page_shape, low) for _, _, _, size in plan]
    if with_cast:
        out_shape.append(jax.ShapeDtypeStruct((share, pages) + page_shape, low))
    out_shape.append(jax.ShapeDtypeStruct((heads, ranks * capacity) + page_shape, low))
    scratch = []
    if with_cast:
        scratch.append(pltpu.VMEM((heads, pages) + page_shape, cache.dtype))
    scratch += [
        pltpu.VMEM((heads, pages + 1) + page_shape, low),
        pltpu.SMEM((ranks * capacity,), jnp.int32),
        pltpu.SMEM((ranks,), jnp.int32),
        pltpu.SemaphoreType.DMA((heads,)),
        pltpu.SemaphoreType.DMA((len(plan),)),
        pltpu.SemaphoreType.DMA,
    ]
    if with_cast:
        scratch.append(pltpu.SemaphoreType.DMA((share,)))
    return pl.pallas_call(
        functools.partial(scatter_kernel, plan, ranks, capacity, pages, with_cast),
        out_shape=out_shape,
        in_specs=[pl.BlockSpec(memory_space=pltpu.SMEM), anywhere],
        out_specs=[anywhere] * len(out_shape),
        scratch_shapes=scratch,
        name="scatter_keys" if with_cast else "scatter_values",
        cost_estimate=pl.CostEstimate(flops=0, bytes_accessed=16 << 20, transcendentals=0),
    )(owner, cache.reshape((heads, pages) + page_shape))


def tail_rows(first, second, dtype):
    rows = lax.broadcasted_iota(jnp.int32, (TAIL, PAGE), 0)
    return jnp.where(rows == 0, first, jnp.where(rows == 1, second, 0.0)).astype(dtype)


def split_mass(mass):
    high = mass.astype(jnp.bfloat16).astype(jnp.float32)
    rows = lax.broadcasted_iota(jnp.int32, mass.shape, 0)
    blocks = mass.shape[0] // 2
    held = jnp.where(rows < blocks // 4, high, 0.0)
    rest = jnp.where(rows < blocks // 4, mass - high, 0.0)
    return (held + pltpu.roll(rest, blocks // 4, 0)).astype(jnp.bfloat16)


def join_mass(tail):
    wide = tail.astype(jnp.float32)
    return wide + pltpu.roll(wide, TAIL - TAIL // 8, 0)


def sweep_kernel(tile, temp_ref, keys_ref, own_ref, other_ref, keep_ref, send_ref, sums_ref, table_ref):
    half, width = own_ref.shape[1:]
    core = lax.axis_index("sub")
    rate = temp_ref[core * pl.num_programs(0) + pl.program_id(0)] * LOG2E
    lane = lax.broadcasted_iota(jnp.int32, (half, width), 1)
    for part, ref in ((0, own_ref), (1, other_ref)):
        table = ref[0]
        norm = -0.5 * jnp.sum(table * table, axis=1, keepdims=True)
        high = norm.astype(jnp.bfloat16).astype(jnp.float32)
        mid = (norm - high).astype(jnp.bfloat16).astype(jnp.float32)
        low = norm - high - mid
        extra = jnp.where(lane == 0, high, jnp.where(lane == 1, mid, jnp.where(lane == 2, low, 0.0)))
        rows = pl.ds(part * half, half)
        table_ref[rows, 0:width] = table.astype(jnp.bfloat16)
        table_ref[rows, width : 2 * width] = extra.astype(jnp.bfloat16)
    sums_ref[...] = jnp.zeros_like(sums_ref)

    def step(at, carry):
        keys = keys_ref[0, pl.ds(pl.multiple_of(at * tile, tile), tile), :]
        wide = jnp.concatenate([keys, jnp.ones_like(keys)], axis=1)
        scores = lax.dot_general(
            table_ref[...], wide, (((1,), (1,)), ((), ())), preferred_element_type=jnp.float32
        )
        highest = jnp.max(scores, axis=0, keepdims=True)
        spread = jnp.exp2((scores - highest) * rate)
        total = jnp.sum(spread, axis=0, keepdims=True)
        weights = (spread * (1.0 / total)).astype(jnp.bfloat16)
        sums_ref[...] += jnp.dot(weights, wide, preferred_element_type=jnp.float32)
        return carry

    lax.fori_loop(0, keys_ref.shape[1] // tile, step, 0, unroll=2)
    masses = []
    for block in range(2 * half // width):
        masses.append(jnp.transpose(sums_ref[pl.ds(block * width, width), width : 2 * width])[0:TAIL])
    keep_ref[0, 0:half] = sums_ref[0:half, 0:width]
    keep_ref[0, half : half + TAIL] = tail_rows(masses[0], masses[1], jnp.float32)
    send_ref[0, 0:half] = sums_ref[half : 2 * half, 0:width].astype(jnp.bfloat16)
    send_ref[0, half : half + TAIL] = split_mass(tail_rows(masses[2], masses[3], jnp.float32))


def sweep(temp, keys, own, other, tile):
    heads, tokens, width = keys.shape
    half = own.shape[1]
    table_spec = pl.BlockSpec((1, half, width), lambda h: (h, 0, 0))
    load_spec = pl.BlockSpec((1, half + TAIL, width), lambda h: (h, 0, 0))
    return pl.pallas_call(
        functools.partial(sweep_kernel, tile),
        grid=(heads,),
        in_specs=[
            pl.BlockSpec(memory_space=pltpu.SMEM),
            pl.BlockSpec((1, tokens, width), lambda h: (h, 0, 0)),
            table_spec,
            table_spec,
        ],
        out_specs=[load_spec, load_spec],
        out_shape=[
            jax.ShapeDtypeStruct((heads, half + TAIL, width), jnp.float32),
            jax.ShapeDtypeStruct((heads, half + TAIL, width), jnp.bfloat16),
        ],
        scratch_shapes=[
            pltpu.VMEM((2 * half, 2 * width), jnp.float32),
            pltpu.VMEM((2 * half, 2 * width), jnp.bfloat16),
        ],
        name="sweep",
        cost_estimate=pl.CostEstimate(
            flops=8 * heads * tokens * half * width, bytes_accessed=2 * heads * tokens * width, transcendentals=2 * heads * tokens * half
        ),
    )(temp, keys, own, other)


def join_kernel(left_ref, right_ref, out_ref):
    half = left_ref.shape[1] - TAIL
    for head in range(left_ref.shape[0]):
        body = left_ref[head, 0:half].astype(jnp.float32) + right_ref[head, 0:half].astype(jnp.float32)
        out_ref[head, 0:half] = body.astype(jnp.bfloat16)
        if left_ref.dtype == jnp.float32:
            mass = left_ref[head, half : half + TAIL]
        else:
            mass = join_mass(left_ref[head, half : half + TAIL])
        mass = mass + join_mass(right_ref[head, half : half + TAIL])
        out_ref[head, half : half + TAIL] = split_mass(mass)


def join(left, right):
    return pl.pallas_call(
        join_kernel,
        out_shape=jax.ShapeDtypeStruct(left.shape, jnp.bfloat16),
        name="join",
    )(left, right)


def renew_kernel(left_ref, right_ref, table_ref, out_ref):
    half, width = table_ref.shape[1:]
    for head in range(left_ref.shape[0]):
        mass = join_mass(left_ref[head, half : half + TAIL]) + join_mass(right_ref[head, half : half + TAIL])
        for block in range(half // width):
            rows = slice(block * width, (block + 1) * width)
            spread = jnp.transpose(jnp.broadcast_to(mass[block : block + 1], (width, width)))
            body = left_ref[head, rows].astype(jnp.float32) + right_ref[head, rows].astype(jnp.float32)
            out_ref[head, rows] = (body + PRIOR * table_ref[head, rows]) / (spread + PRIOR)


def renew(left, right, table):
    return pl.pallas_call(
        renew_kernel,
        out_shape=jax.ShapeDtypeStruct(table.shape, table.dtype),
        name="renew",
    )(left, right, table)


def tied(value, *others):
    return lax.optimization_barrier((value,) + others)


def lower_kernel(cores, cache_ref, *refs):
    ranks = cache_ref.shape[0]
    out_refs, (wide_ref, low_ref, in_sem, out_sem) = refs[:ranks], refs[ranks:]
    part = cache_ref.shape[1] // cores
    first = lax.axis_index("sub") * part
    me = lax.axis_index("seq")
    order = list(range(2, ranks)) + [1, 0]
    for bit in order:
        pltpu.make_async_copy(
            cache_ref.at[me ^ bit, pl.ds(first, part)], wide_ref.at[bit], in_sem.at[bit]
        ).start()
    for bit in order:
        pltpu.make_async_copy(wide_ref.at[bit], wide_ref.at[bit], in_sem.at[bit]).wait()

        def cast(page, carry, bit=bit):
            low_ref[bit, page] = wide_ref[bit, page].astype(low_ref.dtype)
            return carry

        lax.fori_loop(0, part, cast, 0, unroll=2)
        pltpu.make_async_copy(low_ref.at[bit], out_refs[bit], out_sem.at[bit]).start()
    for bit in order:
        pltpu.make_async_copy(low_ref.at[bit], out_refs[bit], out_sem.at[bit]).wait()


def lower_keys(cache, cores):
    ranks, pages = cache.shape[:2]
    part = (pages // cores,) + cache.shape[2:]
    anywhere = pl.BlockSpec(memory_space=pl.ANY)
    return pl.pallas_call(
        functools.partial(lower_kernel, cores),
        out_shape=[jax.ShapeDtypeStruct(part, jnp.bfloat16)] * ranks,
        in_specs=[anywhere],
        out_specs=[anywhere] * ranks,
        scratch_shapes=[
            pltpu.VMEM((ranks,) + part, cache.dtype),
            pltpu.VMEM((ranks,) + part, jnp.bfloat16),
            pltpu.SemaphoreType.DMA((ranks,)),
            pltpu.SemaphoreType.DMA((ranks,)),
        ],
        name="lower_keys",
    )(cache)


def value_heads(me, bit):
    return [0, 1, 2, 3]


def near_pair(me, bit):
    base = ((me ^ 3) >> 1) << 1
    return [base, base + 1]


def near_one(me, bit):
    return [me]


def far_pair(me, bit):
    base = (me >> 1) << 1
    return [base, base + 1]


VALUE_PLAN = ((1, value_heads, 4), (2, value_heads, 4), (3, value_heads, 4))
KEY_PLAN = ((1, near_pair, 2), (1, near_one, 1), (2, far_pair, 2), (3, far_pair, 2))


def pack_kernel(plan, capacity, with_cast, owner_ref, cache_ref, *refs):
    chunk_refs, refs = refs[: len(plan)], refs[len(plan) :]
    if with_cast:
        local_ref, wide_ref, page_ref, table_ref, count_ref, in_sem, chunk_sem, local_sem = refs
    else:
        local_ref, page_ref, table_ref, count_ref, in_sem, chunk_sem, local_sem = refs
    ranks, pages = cache_ref.shape[:2]
    me = lax.axis_index("seq")
    core = lax.axis_index("sub")
    half = capacity // lax.axis_size("sub")
    slots = ranks * capacity
    loads = []
    for head in range(ranks):
        target = wide_ref.at[head] if with_cast else page_ref.at[head, pl.ds(0, pages)]
        load = pltpu.make_async_copy(cache_ref.at[head], target, in_sem.at[head])
        load.start()
        loads.append(load)
    for head in range(ranks):
        page_ref[head, pages] = jnp.zeros(page_ref.shape[2:], page_ref.dtype)
        fill_table(owner_ref, table_ref.at[head], count_ref, head, ranks, capacity, pages)
    for head in range(ranks):
        loads[head].wait()
        if with_cast:

            def cast(page, carry, head=head):
                page_ref[head, page] = wide_ref[head, page].astype(page_ref.dtype)
                return carry

            lax.fori_loop(0, pages, cast, 0, unroll=2)
    for at, (bit, heads_of, _) in enumerate(plan):
        for i, head in enumerate(heads_of(me, bit)):

            def send(slot, carry, at=at, i=i, head=head, bit=bit):
                page = table_ref[head, (me ^ bit) * capacity + core * half + slot]
                pltpu.make_async_copy(page_ref.at[head, page], chunk_refs[at].at[i, slot], chunk_sem.at[at]).start()
                return carry

            lax.fori_loop(0, half, send, 0)
    for head in range(ranks):

        def keep(slot, carry, head=head):
            place = me * capacity + slot
            page = table_ref[head, place]
            pltpu.make_async_copy(page_ref.at[head, page], local_ref.at[head, place], local_sem).start()
            return carry

        lax.fori_loop(0, capacity, keep, 0)
    for at in range(len(plan)):
        pltpu.make_async_copy(chunk_refs[at], chunk_refs[at], chunk_sem.at[at]).wait()
    kept = local_ref.at[:, pl.ds(0, capacity)]
    pltpu.make_async_copy(kept, kept, local_sem).wait()


def pack_pages(owner, cache, plan, capacity, with_cast):
    ranks, pages = cache.shape[:2]
    page_shape = cache.shape[2:]
    half = capacity // lax.axis_size("sub")
    low = jnp.bfloat16
    anywhere = pl.BlockSpec(memory_space=pl.ANY)
    out_shape = [jax.ShapeDtypeStruct((count, half) + page_shape, low) for _, _, count in plan]
    out_shape.append(jax.ShapeDtypeStruct((ranks, ranks * capacity) + page_shape, low))
    scratch = [pltpu.VMEM((ranks, pages) + page_shape, cache.dtype)] if with_cast else []
    scratch += [
        pltpu.VMEM((ranks, pages + 1) + page_shape, low),
        pltpu.SMEM((ranks, ranks * capacity), jnp.int32),
        pltpu.SMEM((ranks,), jnp.int32),
        pltpu.SemaphoreType.DMA((ranks,)),
        pltpu.SemaphoreType.DMA((len(plan),)),
        pltpu.SemaphoreType.DMA,
    ]
    return pl.pallas_call(
        functools.partial(pack_kernel, plan, capacity, with_cast),
        out_shape=out_shape,
        in_specs=[pl.BlockSpec(memory_space=pltpu.SMEM), anywhere],
        out_specs=[anywhere] * len(out_shape),
        scratch_shapes=scratch,
        name="pack_keys" if with_cast else "pack_values",
    )(owner, cache)


def home_kernel(capacity, *refs):
    owner_refs, own_refs, got_refs = refs[0:3], refs[3:6], refs[6:9]
    _, local_ref, next_ref, page_ref, table_ref, in_sem, local_sem, next_sem = refs[9:]
    part = own_refs[0].shape[0]
    pages = part * lax.axis_size("sub")
    me = lax.axis_index("seq")
    core = lax.axis_index("sub")
    for i in range(3):
        pltpu.make_async_copy(own_refs[i], page_ref.at[i, pl.ds(core * part, part)], in_sem.at[i]).start()
        pltpu.make_async_copy(got_refs[i], page_ref.at[i, pl.ds((1 - core) * part, part)], in_sem.at[3 + i]).start()
        page_ref[i, pages] = jnp.zeros(page_ref.shape[2:], page_ref.dtype)

    def clear(slot, carry):
        for row in range(6):
            table_ref[row, slot] = pages
        return carry

    lax.fori_loop(0, capacity, clear, 0)
    for i in range(3):

        def put(page, counts, i=i):
            mine, near = counts
            owner = owner_refs[i][me, page]
            for row, count, wanted in ((i, mine, me), (3 + i, near, me ^ 1)):

                @pl.when(owner == wanted)
                def _(row=row, count=count):
                    table_ref[row, count] = page

            return mine + jnp.where(owner == me, 1, 0), near + jnp.where(owner == (me ^ 1), 1, 0)

        lax.fori_loop(0, pages, put, (jnp.int32(0), jnp.int32(0)))
    for i in range(3):
        whole = page_ref.at[i, pl.ds(0, part)]
        pltpu.make_async_copy(whole, whole, in_sem.at[i]).wait()
        pltpu.make_async_copy(whole, whole, in_sem.at[3 + i]).wait()

    def relay(slot, carry):
        page = table_ref[4 + core, slot]
        pltpu.make_async_copy(page_ref.at[1 + core, page], next_ref.at[slot], next_sem).start()
        return carry

    lax.fori_loop(0, capacity, relay, 0)
    for i in range(3):

        def keep(slot, carry, i=i):
            page = table_ref[i, slot]
            place = (me ^ (i + 1)) * capacity + slot
            pltpu.make_async_copy(page_ref.at[i, page], local_ref.at[me, place], local_sem).start()
            return carry

        lax.fori_loop(0, capacity, keep, 0)
    pltpu.make_async_copy(next_ref, next_ref, next_sem).wait()
    kept = local_ref.at[0, pl.ds(0, 3 * capacity)]
    pltpu.make_async_copy(kept, kept, local_sem).wait()


def home_pages(owners, own, got, local, capacity):
    page_shape = local.shape[2:]
    pages = own[0].shape[0] * lax.axis_size("sub")
    anywhere = pl.BlockSpec(memory_space=pl.ANY)
    return pl.pallas_call(
        functools.partial(home_kernel, capacity),
        out_shape=[
            jax.ShapeDtypeStruct(local.shape, local.dtype),
            jax.ShapeDtypeStruct((capacity,) + page_shape, local.dtype),
        ],
        in_specs=[pl.BlockSpec(memory_space=pltpu.SMEM)] * 3 + [anywhere] * 7,
        out_specs=[anywhere] * 2,
        scratch_shapes=[
            pltpu.VMEM((3, pages + 1) + page_shape, local.dtype),
            pltpu.SMEM((6, capacity), jnp.int32),
            pltpu.SemaphoreType.DMA((6,)),
            pltpu.SemaphoreType.DMA,
            pltpu.SemaphoreType.DMA,
        ],
        input_output_aliases={9: 0},
        name="home_pages",
    )(*owners, *own, *got, local)


def home_sweep_kernel(tile, temp_ref, *refs):
    key_refs, (center_ref, out_ref, sums_ref, table_ref) = refs[:-4], refs[-4:]
    count, width = center_ref.shape
    rate = temp_ref[lax.axis_index("seq")] * LOG2E
    table = center_ref[...]
    lane = lax.broadcasted_iota(jnp.int32, table.shape, 1)
    norm = -0.5 * jnp.sum(table * table, axis=1, keepdims=True)
    high = norm.astype(jnp.bfloat16).astype(jnp.float32)
    mid = (norm - high).astype(jnp.bfloat16).astype(jnp.float32)
    low = norm - high - mid
    extra = jnp.where(lane == 0, high, jnp.where(lane == 1, mid, jnp.where(lane == 2, low, 0.0)))
    table_ref[:, 0:width] = table.astype(jnp.bfloat16)
    table_ref[:, width : 2 * width] = extra.astype(jnp.bfloat16)
    sums_ref[...] = jnp.zeros_like(sums_ref)
    for keys_ref in key_refs:

        def step(at, carry, keys_ref=keys_ref):
            keys = keys_ref[pl.ds(pl.multiple_of(at * tile, tile), tile), :]
            wide = jnp.concatenate([keys, jnp.ones_like(keys)], axis=1)
            scores = lax.dot_general(
                table_ref[...], wide, (((1,), (1,)), ((), ())), preferred_element_type=jnp.float32
            )
            highest = jnp.max(scores, axis=0, keepdims=True)
            spread = jnp.exp2((scores - highest) * rate)
            total = jnp.sum(spread, axis=0, keepdims=True)
            weights = (spread * (1.0 / total)).astype(jnp.bfloat16)
            sums_ref[...] += jnp.dot(weights, wide, preferred_element_type=jnp.float32)
            return carry

        lax.fori_loop(0, keys_ref.shape[0] // tile, step, 0, unroll=2)
    out_ref[0:count] = sums_ref[:, 0:width]
    rows = lax.broadcasted_iota(jnp.int32, (TAIL, width), 0)
    tail = jnp.zeros((TAIL, width), jnp.float32)
    for block in range(count // width):
        mass = jnp.transpose(sums_ref[pl.ds(block * width, width), width : 2 * width])[0:TAIL]
        tail = jnp.where(rows == block, mass, tail)
    out_ref[count : count + TAIL] = tail


def home_sweep(temp, keys, table, tile):
    count, width = table.shape
    vmem = pl.BlockSpec(memory_space=pltpu.VMEM)
    return pl.pallas_call(
        functools.partial(home_sweep_kernel, tile),
        out_shape=jax.ShapeDtypeStruct((count + TAIL, width), jnp.float32),
        in_specs=[pl.BlockSpec(memory_space=pltpu.SMEM)] + [vmem] * (len(keys) + 1),
        out_specs=vmem,
        scratch_shapes=[
            pltpu.VMEM((count, 2 * width), jnp.float32),
            pltpu.VMEM((count, 2 * width), jnp.bfloat16),
        ],
        name="home_sweep",
    )(temp, *keys, table)


def home_renew_kernel(left_ref, right_ref, table_ref, out_ref):
    count, width = table_ref.shape
    mass = left_ref[count : count + TAIL] + right_ref[count : count + TAIL]
    for block in range(count // width):
        rows = slice(block * width, (block + 1) * width)
        spread = jnp.transpose(jnp.broadcast_to(mass[block : block + 1], (width, width)))
        body = left_ref[rows] + right_ref[rows]
        out_ref[rows] = (body + PRIOR * table_ref[rows]) / (spread + PRIOR)


def home_renew(left, right, table):
    return pl.pallas_call(
        home_renew_kernel, out_shape=jax.ShapeDtypeStruct(table.shape, table.dtype), name="home_renew"
    )(left, right, table)


def on_home_chips(key_cache, value_cache, centroids, inv_temp, page_owner):
    heads, tokens, width = key_cache.shape
    pages = tokens // PAGE
    ranks, cores = lax.axis_size("seq"), lax.axis_size("sub")
    me, core = lax.axis_index("seq"), lax.axis_index("sub")
    capacity = max(2, (3 * pages + 2 * ranks - 1) // (2 * ranks))
    half = capacity // cores
    owner = page_owner[:, :, 0]
    paged = (heads, pages, PAGE, width)
    across = lambda value: lax.ppermute(value, "sub", [(0, 1), (1, 0)])
    facing = lambda value, bit: lax.ppermute(value, "seq", [(i, i ^ bit) for i in range(ranks)])

    lowered = lower_keys(key_cache.reshape(paged), cores)
    homed = [lowered[0]] + [None] * 3
    for bit in (2, 3, 1):
        homed[bit] = facing(lowered[bit], bit)

    owner_after, value_after = tied(owner, value_cache, lowered[1])[:2]
    *value_chunks, moved_values = pack_pages(owner_after, value_after.reshape(paged), VALUE_PLAN, capacity, False)
    values_in = [facing(chunk, spec[0]) for chunk, spec in zip(value_chunks, VALUE_PLAN)]

    owner_after, key_after = tied(owner, key_cache, value_chunks[0])[:2]
    owners = [owner] + [facing(owner_after, bit) for bit in range(1, ranks)]
    *key_chunks, moved_keys = pack_pages(owner_after, key_after.reshape(paged), KEY_PLAN, capacity, True)
    keys_in = [facing(chunk, spec[0]) for chunk, spec in zip(key_chunks[:-1], KEY_PLAN)]

    seeds = lax.dynamic_index_in_dim(centroids, me, 0, keepdims=False)
    seeds_got = across(seeds)
    table = jnp.where(
        core == 0, jnp.concatenate([seeds, seeds_got], axis=0), jnp.concatenate([seeds_got, seeds], axis=0)
    )
    keys = [part.reshape(part.shape[0] * PAGE, width) for part in homed]
    for iteration in range(ITERS):
        sums = home_sweep(inv_temp, keys, table, 512)
        if iteration == 0:
            homed_got = [across(homed[bit]) for bit in (1, 2, 3)]
            moved_keys, relayed = home_pages(owners[1:], homed[1:], homed_got, moved_keys, capacity)
            relayed_in = facing(relayed, 1)
        table = home_renew(sums, across(sums), table)

    ours = lax.dynamic_slice_in_dim(table, core * (table.shape[0] // cores), table.shape[0] // cores, 0)
    opposite = facing(ours, 2)
    last, _ = tied(key_chunks[-1], table)
    keys_in.append(facing(last, KEY_PLAN[-1][0]))
    near = facing(jnp.stack([ours, opposite]), 1)

    def place(whole, part, head, slot):
        return lax.dynamic_update_slice(whole, part, (head, slot, 0, 0))

    for (bit, heads_of, _), part in zip(VALUE_PLAN, values_in):
        part, _ = tied(part, table)
        base = (me ^ bit) * capacity
        moved_values = place(moved_values, part, 0, base + core * half)
        moved_values = place(moved_values, across(part), 0, base + (1 - core) * half)
    relayed_in, _ = tied(relayed_in, table)
    for part, side in ((relayed_in, core), (across(relayed_in), 1 - core)):
        moved_keys = place(moved_keys, part[None], me ^ 1, (me ^ 3 ^ side) * capacity)
    for (bit, heads_of, _), part in zip(KEY_PLAN, keys_in):
        part, _ = tied(part, table)
        base = (me ^ bit) * capacity
        head = heads_of(me ^ bit, bit)[0]
        moved_keys = place(moved_keys, part, head, base + core * half)
        moved_keys = place(moved_keys, across(part), head, base + (1 - core) * half)

    clusters = jnp.zeros(centroids.shape, centroids.dtype)
    for part, head in ((ours, me), (opposite, me ^ 2), (near[0], me ^ 1), (near[1], me ^ 3)):
        clusters = lax.dynamic_update_slice(clusters, part[None], (head, 0, 0))
    sources = [me ^ bit for bit in range(ranks)]
    return (clusters, moved_keys, moved_values, slot_pages(owners, sources, pages, capacity))


def slot_pages(owners, sources, pages, capacity):
    me = lax.axis_index("seq")
    slot_ids = jnp.arange(capacity, dtype=jnp.int32)
    heads = owners[0].shape[0]
    ids = jnp.full((heads, len(owners) * capacity), -1, jnp.int32)
    for owner, source in zip(owners, sources):
        hits = (owner == me).astype(jnp.int32)
        before = jnp.cumsum(hits, axis=1) - hits
        matched = (hits[:, None, :] == 1) & (before[:, None, :] == slot_ids[None, :, None])
        number = source * pages + jnp.arange(pages, dtype=jnp.int32)
        found = jnp.max(jnp.where(matched, number[None, None, :], -1), axis=2)
        ids = lax.dynamic_update_slice(ids, found, (0, source * capacity))
    return ids


def on_device(key_cache, value_cache, centroids, inv_temp, page_owner):
    heads, tokens, width = key_cache.shape
    pages = tokens // PAGE
    ranks = lax.axis_size("seq")
    cores = lax.axis_size("sub")
    me, core = lax.axis_index("seq"), lax.axis_index("sub")
    share = heads // cores
    capacity = max(2, (3 * pages + 2 * ranks - 1) // (2 * ranks))
    owner = page_owner[:, :, 0]
    swap = [(0, 1), (1, 0)]
    ring = lambda shift: [(i, (i + shift) % ranks) for i in range(ranks)]
    facing = lambda bit: [(i, i ^ bit) for i in range(ranks)]

    owners = [owner] + [lax.ppermute(owner, "seq", ring(shift)) for shift in range(1, ranks)]

    mine = lax.dynamic_slice_in_dim(centroids, core * share, share, 0)
    theirs = lax.dynamic_slice_in_dim(centroids, (1 - core) * share, share, 0)
    got = lax.ppermute(theirs, "sub", swap)
    straight = lax.rem(me, 2) == core
    own = jnp.where(straight, mine, got)
    other = jnp.where(straight, got, mine)

    plan = chunk_plan(ranks, share, capacity)
    *value_chunks, moved_values = scatter_pages(owner, value_cache, plan, ranks, capacity, False)
    *key_chunks, keys_low, moved_keys = scatter_pages(owner, key_cache, plan, ranks, capacity, True)
    keys_low = keys_low.reshape(share, tokens, width)

    waiting = [(0, spec, chunk) for spec, chunk in zip(plan, value_chunks)]
    waiting += [(1, spec, chunk) for spec, chunk in zip(plan, key_chunks)]
    moved = [moved_values, moved_keys]
    arrived = []

    def issue(count, after=None):
        for _ in range(count):
            if not waiting:
                return
            which, spec, chunk = waiting.pop(0)
            if after is not None:
                chunk, _ = tied(chunk, after)
            arrived.append((which, spec, lax.ppermute(chunk, "seq", ring(spec[0]))))

    stages = ITERS * (1 + ranks.bit_length())
    per_stage = -(-len(waiting) // (stages + 1))
    issue(2)
    for iteration in range(ITERS):
        keep, send = sweep(inv_temp, keys_low, own, other, 512)
        got = lax.ppermute(send, "seq", facing(1))
        issue(per_stage, send)
        payload = join(keep, got)
        bit = 2
        while bit < ranks:
            got = lax.ppermute(payload, "seq", facing(bit))
            issue(per_stage, payload)
            bit *= 2
            if bit < ranks:
                payload = join(payload, got)
        own = renew(payload, got, own)
        other = lax.ppermute(own, "seq", facing(1))
        issue(per_stage, own)
    issue(len(waiting))

    for which, (shift, head, first, size), chunk in arrived:
        partner = lax.ppermute(chunk, "sub", swap)
        start = lax.rem(me - shift + ranks, ranks) * capacity + first
        place = lambda whole, part, at: lax.dynamic_update_slice(whole, part[None], (at, start, 0, 0))
        moved[which] = place(moved[which], chunk, core * share + head)
        moved[which] = place(moved[which], partner, (1 - core) * share + head)

    lower = jnp.where(lax.rem(me, 2) == 0, own, other)
    upper = jnp.where(lax.rem(me, 2) == 0, other, own)
    ours = jnp.where(core == 0, lower, upper)
    other_half = lax.ppermute(jnp.where(core == 0, upper, lower), "sub", swap)
    clusters = jnp.where(
        core == 0, jnp.concatenate([ours, other_half], axis=0), jnp.concatenate([other_half, ours], axis=0)
    )

    sources = [lax.rem(me - shift + ranks, ranks) for shift in range(ranks)]
    ids = slot_pages(owners, sources, pages, capacity)
    return (clusters, moved[1], moved[0], ids)


def choose(key_cache, value_cache, centroids, inv_temp, page_owner):
    ranks, cores = lax.axis_size("seq"), lax.axis_size("sub")
    homes = ranks == 4 and key_cache.shape[0] == ranks and cores == 2
    body = on_home_chips if homes else on_device
    return body(key_cache, value_cache, centroids, inv_temp, page_owner)


def solution(mesh):
    return jax.shard_map(
        choose,
        mesh=mesh,
        in_specs=(
            P("head", ("rep", "seq"), None),
            P("head", ("rep", "seq"), None),
            P("head", ("rep", "sub"), None),
            P("head"),
            P("head", ("rep", "seq"), None),
        ),
        out_specs=(
            P("head", ("rep", "sub"), None),
            P("head", ("rep", "seq"), None, None),
            P("head", ("rep", "seq"), None, None),
            P("head", ("rep", "seq")),
        ),
        check_vma=False,
    )
```

```python
import functools

import jax
import jax.numpy as jnp
from jax import lax
from jax.experimental import pallas as pl
from jax.experimental.pallas import tpu as pltpu
from jax.sharding import PartitionSpec as P


ITERS = 3
PAGE = 128
PRIOR = 8.0
TAIL = 16
LOG2E = 1.4426950408889634


def chunk_plan(ranks, heads, capacity):
    plan = []
    for head in range(heads):
        for shift in range(1, ranks):
            crossing = min(shift, ranks - shift)
            pieces = crossing if capacity % crossing == 0 else 1
            for piece in range(pieces):
                plan.append((shift, head, piece * (capacity // pieces), capacity // pieces))
    return plan


def fill_table(owner_ref, table_ref, count_ref, head, ranks, capacity, pages):
    def clear(slot, carry):
        table_ref[slot] = pages
        return carry

    lax.fori_loop(0, ranks * capacity, clear, 0)
    for rank in range(ranks):
        count_ref[rank] = 0

    def put(page, carry):
        owner = owner_ref[head, page]
        place = count_ref[owner]
        table_ref[owner * capacity + place] = page
        count_ref[owner] = place + 1
        return carry

    lax.fori_loop(0, pages, put, 0)


def scatter_kernel(plan, ranks, capacity, pages, with_cast, owner_ref, cache_ref, *refs):
    chunk_refs, refs = refs[: len(plan)], refs[len(plan) :]
    if with_cast:
        low_ref, local_ref, wide_ref, page_ref, table_ref, count_ref, in_sem, chunk_sem, local_sem, low_sem = refs
    else:
        local_ref, page_ref, table_ref, count_ref, in_sem, chunk_sem, local_sem = refs
    heads = cache_ref.shape[0]
    me = lax.axis_index("seq")
    core = lax.axis_index("sub")
    share = heads // lax.axis_size("sub")
    order = [(core * share + i) for i in range(share)]
    order += [lax.rem(core * share + i, heads) for i in range(share, heads)]
    into = wide_ref if with_cast else page_ref
    loads = []
    for i, head in enumerate(order):
        target = into.at[i] if with_cast else into.at[i, pl.ds(0, pages)]
        load = pltpu.make_async_copy(cache_ref.at[head], target, in_sem.at[i])
        load.start()
        loads.append(load)
    for i in range(heads):
        page_ref[i, pages] = jnp.zeros(page_ref.shape[2:], page_ref.dtype)
    for i, head in enumerate(order):
        fill_table(owner_ref, table_ref, count_ref, head, ranks, capacity, pages)
        loads[i].wait()
        if with_cast:

            def cast(page, carry, i=i):
                page_ref[i, page] = wide_ref[i, page].astype(page_ref.dtype)
                return carry

            lax.fori_loop(0, pages, cast, 0, unroll=2)
            if i < share:
                pltpu.make_async_copy(page_ref.at[i, pl.ds(0, pages)], low_ref.at[i], low_sem.at[i]).start()
        for j, (shift, chunk_head, first, size) in enumerate(plan):
            if chunk_head != i:
                continue
            base = lax.rem(me + shift, ranks) * capacity + first

            def send(slot, carry, i=i, j=j, base=base):
                page = table_ref[base + slot]
                pltpu.make_async_copy(page_ref.at[i, page], chunk_refs[j].at[slot], chunk_sem.at[j]).start()
                return carry

            lax.fori_loop(0, size, send, 0)

        def keep(slot, carry, i=i, head=head):
            place = me * capacity + slot
            page = table_ref[place]
            pltpu.make_async_copy(page_ref.at[i, page], local_ref.at[head, place], local_sem).start()
            return carry

        lax.fori_loop(0, capacity, keep, 0)
    for j in range(len(plan)):
        pltpu.make_async_copy(chunk_refs[j], chunk_refs[j], chunk_sem.at[j]).wait()
    if with_cast:
        for i in range(share):
            pltpu.make_async_copy(low_ref.at[i], low_ref.at[i], low_sem.at[i]).wait()
    kept = local_ref.at[:, pl.ds(0, capacity)]
    pltpu.make_async_copy(kept, kept, local_sem).wait()


def scatter_pages(owner, cache, plan, ranks, capacity, with_cast):
    heads, tokens, width = cache.shape
    pages = tokens // PAGE
    share = heads // lax.axis_size("sub")
    page_shape = (PAGE, width)
    low = jnp.bfloat16
    anywhere = pl.BlockSpec(memory_space=pl.ANY)
    out_shape = [jax.ShapeDtypeStruct((size,) + page_shape, low) for _, _, _, size in plan]
    if with_cast:
        out_shape.append(jax.ShapeDtypeStruct((share, pages) + page_shape, low))
    out_shape.append(jax.ShapeDtypeStruct((heads, ranks * capacity) + page_shape, low))
    scratch = []
    if with_cast:
        scratch.append(pltpu.VMEM((heads, pages) + page_shape, cache.dtype))
    scratch += [
        pltpu.VMEM((heads, pages + 1) + page_shape, low),
        pltpu.SMEM((ranks * capacity,), jnp.int32),
        pltpu.SMEM((ranks,), jnp.int32),
        pltpu.SemaphoreType.DMA((heads,)),
        pltpu.SemaphoreType.DMA((len(plan),)),
        pltpu.SemaphoreType.DMA,
    ]
    if with_cast:
        scratch.append(pltpu.SemaphoreType.DMA((share,)))
    return pl.pallas_call(
        functools.partial(scatter_kernel, plan, ranks, capacity, pages, with_cast),
        out_shape=out_shape,
        in_specs=[pl.BlockSpec(memory_space=pltpu.SMEM), anywhere],
        out_specs=[anywhere] * len(out_shape),
        scratch_shapes=scratch,
        name="scatter_keys" if with_cast else "scatter_values",
        cost_estimate=pl.CostEstimate(flops=0, bytes_accessed=16 << 20, transcendentals=0),
    )(owner, cache.reshape((heads, pages) + page_shape))


def tail_rows(first, second, dtype):
    rows = lax.broadcasted_iota(jnp.int32, (TAIL, PAGE), 0)
    return jnp.where(rows == 0, first, jnp.where(rows == 1, second, 0.0)).astype(dtype)


def split_mass(mass):
    high = mass.astype(jnp.bfloat16).astype(jnp.float32)
    rows = lax.broadcasted_iota(jnp.int32, mass.shape, 0)
    blocks = mass.shape[0] // 2
    held = jnp.where(rows < blocks // 4, high, 0.0)
    rest = jnp.where(rows < blocks // 4, mass - high, 0.0)
    return (held + pltpu.roll(rest, blocks // 4, 0)).astype(jnp.bfloat16)


def join_mass(tail):
    wide = tail.astype(jnp.float32)
    return wide + pltpu.roll(wide, TAIL - TAIL // 8, 0)


def sweep_kernel(tile, temp_ref, keys_ref, own_ref, other_ref, keep_ref, send_ref, sums_ref, table_ref):
    half, width = own_ref.shape[1:]
    core = lax.axis_index("sub")
    rate = temp_ref[core * pl.num_programs(0) + pl.program_id(0)] * LOG2E
    lane = lax.broadcasted_iota(jnp.int32, (half, width), 1)
    for part, ref in ((0, own_ref), (1, other_ref)):
        table = ref[0]
        norm = -0.5 * jnp.sum(table * table, axis=1, keepdims=True)
        high = norm.astype(jnp.bfloat16).astype(jnp.float32)
        mid = (norm - high).astype(jnp.bfloat16).astype(jnp.float32)
        low = norm - high - mid
        extra = jnp.where(lane == 0, high, jnp.where(lane == 1, mid, jnp.where(lane == 2, low, 0.0)))
        rows = pl.ds(part * half, half)
        table_ref[rows, 0:width] = table.astype(jnp.bfloat16)
        table_ref[rows, width : 2 * width] = extra.astype(jnp.bfloat16)
    sums_ref[...] = jnp.zeros_like(sums_ref)

    def step(at, carry):
        keys = keys_ref[0, pl.ds(pl.multiple_of(at * tile, tile), tile), :]
        wide = jnp.concatenate([keys, jnp.ones_like(keys)], axis=1)
        scores = lax.dot_general(
            table_ref[...], wide, (((1,), (1,)), ((), ())), preferred_element_type=jnp.float32
        )
        highest = jnp.max(scores, axis=0, keepdims=True)
        spread = jnp.exp2((scores - highest) * rate)
        total = jnp.sum(spread, axis=0, keepdims=True)
        weights = (spread * (1.0 / total)).astype(jnp.bfloat16)
        sums_ref[...] += jnp.dot(weights, wide, preferred_element_type=jnp.float32)
        return carry

    lax.fori_loop(0, keys_ref.shape[1] // tile, step, 0, unroll=2)
    masses = []
    for block in range(2 * half // width):
        masses.append(jnp.transpose(sums_ref[pl.ds(block * width, width), width : 2 * width])[0:TAIL])
    keep_ref[0, 0:half] = sums_ref[0:half, 0:width]
    keep_ref[0, half : half + TAIL] = tail_rows(masses[0], masses[1], jnp.float32)
    send_ref[0, 0:half] = sums_ref[half : 2 * half, 0:width].astype(jnp.bfloat16)
    send_ref[0, half : half + TAIL] = split_mass(tail_rows(masses[2], masses[3], jnp.float32))


def sweep(temp, keys, own, other, tile):
    heads, tokens, width = keys.shape
    half = own.shape[1]
    table_spec = pl.BlockSpec((1, half, width), lambda h: (h, 0, 0))
    load_spec = pl.BlockSpec((1, half + TAIL, width), lambda h: (h, 0, 0))
    return pl.pallas_call(
        functools.partial(sweep_kernel, tile),
        grid=(heads,),
        in_specs=[
            pl.BlockSpec(memory_space=pltpu.SMEM),
            pl.BlockSpec((1, tokens, width), lambda h: (h, 0, 0)),
            table_spec,
            table_spec,
        ],
        out_specs=[load_spec, load_spec],
        out_shape=[
            jax.ShapeDtypeStruct((heads, half + TAIL, width), jnp.float32),
            jax.ShapeDtypeStruct((heads, half + TAIL, width), jnp.bfloat16),
        ],
        scratch_shapes=[
            pltpu.VMEM((2 * half, 2 * width), jnp.float32),
            pltpu.VMEM((2 * half, 2 * width), jnp.bfloat16),
        ],
        name="sweep",
        cost_estimate=pl.CostEstimate(
            flops=8 * heads * tokens * half * width, bytes_accessed=2 * heads * tokens * width, transcendentals=2 * heads * tokens * half
        ),
    )(temp, keys, own, other)


def join_kernel(left_ref, right_ref, out_ref):
    half = left_ref.shape[1] - TAIL
    for head in range(left_ref.shape[0]):
        body = left_ref[head, 0:half].astype(jnp.float32) + right_ref[head, 0:half].astype(jnp.float32)
        out_ref[head, 0:half] = body.astype(jnp.bfloat16)
        if left_ref.dtype == jnp.float32:
            mass = left_ref[head, half : half + TAIL]
        else:
            mass = join_mass(left_ref[head, half : half + TAIL])
        mass = mass + join_mass(right_ref[head, half : half + TAIL])
        out_ref[head, half : half + TAIL] = split_mass(mass)


def join(left, right):
    return pl.pallas_call(
        join_kernel,
        out_shape=jax.ShapeDtypeStruct(left.shape, jnp.bfloat16),
        name="join",
    )(left, right)


def renew_kernel(left_ref, right_ref, table_ref, out_ref):
    half, width = table_ref.shape[1:]
    for head in range(left_ref.shape[0]):
        mass = join_mass(left_ref[head, half : half + TAIL]) + join_mass(right_ref[head, half : half + TAIL])
        for block in range(half // width):
            rows = slice(block * width, (block + 1) * width)
            spread = jnp.transpose(jnp.broadcast_to(mass[block : block + 1], (width, width)))
            body = left_ref[head, rows].astype(jnp.float32) + right_ref[head, rows].astype(jnp.float32)
            out_ref[head, rows] = (body + PRIOR * table_ref[head, rows]) / (spread + PRIOR)


def renew(left, right, table):
    return pl.pallas_call(
        renew_kernel,
        out_shape=jax.ShapeDtypeStruct(table.shape, table.dtype),
        name="renew",
    )(left, right, table)


def tied(value, *others):
    return lax.optimization_barrier((value,) + others)


def lower_kernel(cores, cache_ref, *refs):
    ranks = cache_ref.shape[0]
    out_refs, (wide_ref, low_ref, in_sem, out_sem) = refs[:ranks], refs[ranks:]
    part = cache_ref.shape[1] // cores
    first = lax.axis_index("sub") * part
    me = lax.axis_index("seq")
    order = list(range(1, ranks)) + [0]
    for bit in order:
        pltpu.make_async_copy(
            cache_ref.at[me ^ bit, pl.ds(first, part)], wide_ref.at[bit], in_sem.at[bit]
        ).start()
    for bit in order:
        pltpu.make_async_copy(wide_ref.at[bit], wide_ref.at[bit], in_sem.at[bit]).wait()

        def cast(page, carry, bit=bit):
            low_ref[bit, page] = wide_ref[bit, page].astype(low_ref.dtype)
            return carry

        lax.fori_loop(0, part, cast, 0, unroll=2)
        pltpu.make_async_copy(low_ref.at[bit], out_refs[bit], out_sem.at[bit]).start()
    for bit in order:
        pltpu.make_async_copy(low_ref.at[bit], out_refs[bit], out_sem.at[bit]).wait()


def lower_keys(cache, cores):
    ranks, pages = cache.shape[:2]
    part = (pages // cores,) + cache.shape[2:]
    anywhere = pl.BlockSpec(memory_space=pl.ANY)
    return pl.pallas_call(
        functools.partial(lower_kernel, cores),
        out_shape=[jax.ShapeDtypeStruct(part, jnp.bfloat16)] * ranks,
        in_specs=[anywhere],
        out_specs=[anywhere] * ranks,
        scratch_shapes=[
            pltpu.VMEM((ranks,) + part, cache.dtype),
            pltpu.VMEM((ranks,) + part, jnp.bfloat16),
            pltpu.SemaphoreType.DMA((ranks,)),
            pltpu.SemaphoreType.DMA((ranks,)),
        ],
        name="lower_keys",
    )(cache)


def value_heads(me, bit):
    return [0, 1, 2, 3]


def near_pair(me, bit):
    base = ((me ^ 3) >> 1) << 1
    return [base, base + 1]


def near_one(me, bit):
    return [me]


def far_pair(me, bit):
    base = (me >> 1) << 1
    return [base, base + 1]


VALUE_PLAN = ((1, value_heads, 4), (2, value_heads, 4), (3, value_heads, 4))
KEY_PLAN = ((1, near_pair, 2), (1, near_one, 1), (2, far_pair, 2), (3, far_pair, 2))


def pack_kernel(plan, capacity, with_cast, owner_ref, cache_ref, *refs):
    chunk_refs, refs = refs[: len(plan)], refs[len(plan) :]
    if with_cast:
        local_ref, wide_ref, page_ref, table_ref, count_ref, in_sem, chunk_sem, local_sem = refs
    else:
        local_ref, page_ref, table_ref, count_ref, in_sem, chunk_sem, local_sem = refs
    ranks, pages = cache_ref.shape[:2]
    me = lax.axis_index("seq")
    core = lax.axis_index("sub")
    half = capacity // lax.axis_size("sub")
    loads = []
    for head in range(ranks):
        target = wide_ref.at[head] if with_cast else page_ref.at[head, pl.ds(0, pages)]
        load = pltpu.make_async_copy(cache_ref.at[head], target, in_sem.at[head])
        load.start()
        loads.append(load)
    for head in range(ranks):
        page_ref[head, pages] = jnp.zeros(page_ref.shape[2:], page_ref.dtype)
        fill_table(owner_ref, table_ref.at[head], count_ref, head, ranks, capacity, pages)
    for head in range(ranks):
        loads[head].wait()
        if with_cast:

            def cast(page, carry, head=head):
                page_ref[head, page] = wide_ref[head, page].astype(page_ref.dtype)
                return carry

            lax.fori_loop(0, pages, cast, 0, unroll=2)
    for at, (bit, heads_of, _) in enumerate(plan):
        for i, head in enumerate(heads_of(me, bit)):

            def send(slot, carry, at=at, i=i, head=head, bit=bit):
                page = table_ref[head, (me ^ bit) * capacity + core * half + slot]
                pltpu.make_async_copy(page_ref.at[head, page], chunk_refs[at].at[i, slot], chunk_sem.at[at]).start()
                return carry

            lax.fori_loop(0, half, send, 0)
    for head in range(ranks):

        def keep(slot, carry, head=head):
            place = me * capacity + slot
            page = table_ref[head, place]
            pltpu.make_async_copy(page_ref.at[head, page], local_ref.at[head, place], local_sem).start()
            return carry

        lax.fori_loop(0, capacity, keep, 0)
    for at in range(len(plan)):
        pltpu.make_async_copy(chunk_refs[at], chunk_refs[at], chunk_sem.at[at]).wait()
    kept = local_ref.at[:, pl.ds(0, capacity)]
    pltpu.make_async_copy(kept, kept, local_sem).wait()


def pack_pages(owner, cache, plan, capacity, with_cast):
    ranks, pages = cache.shape[:2]
    page_shape = cache.shape[2:]
    half = capacity // lax.axis_size("sub")
    low = jnp.bfloat16
    anywhere = pl.BlockSpec(memory_space=pl.ANY)
    out_shape = [jax.ShapeDtypeStruct((count, half) + page_shape, low) for _, _, count in plan]
    out_shape.append(jax.ShapeDtypeStruct((ranks, ranks * capacity) + page_shape, low))
    scratch = [pltpu.VMEM((ranks, pages) + page_shape, cache.dtype)] if with_cast else []
    scratch += [
        pltpu.VMEM((ranks, pages + 1) + page_shape, low),
        pltpu.SMEM((ranks, ranks * capacity), jnp.int32),
        pltpu.SMEM((ranks,), jnp.int32),
        pltpu.SemaphoreType.DMA((ranks,)),
        pltpu.SemaphoreType.DMA((len(plan),)),
        pltpu.SemaphoreType.DMA,
    ]
    return pl.pallas_call(
        functools.partial(pack_kernel, plan, capacity, with_cast),
        out_shape=out_shape,
        in_specs=[pl.BlockSpec(memory_space=pltpu.SMEM), anywhere],
        out_specs=[anywhere] * len(out_shape),
        scratch_shapes=scratch,
        name="pack_keys" if with_cast else "pack_values",
    )(owner, cache)


def home_kernel(capacity, *refs):
    owner_refs, own_refs, got_refs = refs[0:3], refs[3:6], refs[6:9]
    _, local_ref, next_ref, page_ref, table_ref, in_sem, local_sem, next_sem = refs[9:]
    part = own_refs[0].shape[0]
    pages = part * lax.axis_size("sub")
    me = lax.axis_index("seq")
    core = lax.axis_index("sub")
    for i in range(3):
        pltpu.make_async_copy(own_refs[i], page_ref.at[i, pl.ds(core * part, part)], in_sem.at[i]).start()
        pltpu.make_async_copy(got_refs[i], page_ref.at[i, pl.ds((1 - core) * part, part)], in_sem.at[3 + i]).start()
        page_ref[i, pages] = jnp.zeros(page_ref.shape[2:], page_ref.dtype)

    def clear(slot, carry):
        for row in range(6):
            table_ref[row, slot] = pages
        return carry

    lax.fori_loop(0, capacity, clear, 0)
    for i in range(3):

        def put(page, counts, i=i):
            mine, near = counts
            owner = owner_refs[i][me, page]
            for row, count, wanted in ((i, mine, me), (3 + i, near, me ^ 1)):

                @pl.when(owner == wanted)
                def _(row=row, count=count):
                    table_ref[row, count] = page

            return mine + jnp.where(owner == me, 1, 0), near + jnp.where(owner == (me ^ 1), 1, 0)

        lax.fori_loop(0, pages, put, (jnp.int32(0), jnp.int32(0)))
    for i in range(3):
        whole = page_ref.at[i, pl.ds(0, part)]
        pltpu.make_async_copy(whole, whole, in_sem.at[i]).wait()
        pltpu.make_async_copy(whole, whole, in_sem.at[3 + i]).wait()

    def relay(slot, carry):
        page = table_ref[4 + core, slot]
        pltpu.make_async_copy(page_ref.at[1 + core, page], next_ref.at[slot], next_sem).start()
        return carry

    lax.fori_loop(0, capacity, relay, 0)
    for i in range(3):

        def keep(slot, carry, i=i):
            page = table_ref[i, slot]
            place = (me ^ (i + 1)) * capacity + slot
            pltpu.make_async_copy(page_ref.at[i, page], local_ref.at[me, place], local_sem).start()
            return carry

        lax.fori_loop(0, capacity, keep, 0)
    pltpu.make_async_copy(next_ref, next_ref, next_sem).wait()
    kept = local_ref.at[0, pl.ds(0, 3 * capacity)]
    pltpu.make_async_copy(kept, kept, local_sem).wait()


def home_pages(owners, own, got, local, capacity):
    page_shape = local.shape[2:]
    pages = own[0].shape[0] * lax.axis_size("sub")
    anywhere = pl.BlockSpec(memory_space=pl.ANY)
    return pl.pallas_call(
        functools.partial(home_kernel, capacity),
        out_shape=[
            jax.ShapeDtypeStruct(local.shape, local.dtype),
            jax.ShapeDtypeStruct((capacity,) + page_shape, local.dtype),
        ],
        in_specs=[pl.BlockSpec(memory_space=pltpu.SMEM)] * 3 + [anywhere] * 7,
        out_specs=[anywhere] * 2,
        scratch_shapes=[
            pltpu.VMEM((3, pages + 1) + page_shape, local.dtype),
            pltpu.SMEM((6, capacity), jnp.int32),
            pltpu.SemaphoreType.DMA((6,)),
            pltpu.SemaphoreType.DMA,
            pltpu.SemaphoreType.DMA,
        ],
        input_output_aliases={9: 0},
        name="home_pages",
    )(*owners, *own, *got, local)


def home_sweep_kernel(tile, temp_ref, *refs):
    key_refs, (center_ref, out_ref, sums_ref, table_ref) = refs[:-4], refs[-4:]
    count, width = center_ref.shape
    rate = temp_ref[lax.axis_index("seq")] * LOG2E
    table = center_ref[...]
    lane = lax.broadcasted_iota(jnp.int32, table.shape, 1)
    norm = -0.5 * jnp.sum(table * table, axis=1, keepdims=True)
    high = norm.astype(jnp.bfloat16).astype(jnp.float32)
    mid = (norm - high).astype(jnp.bfloat16).astype(jnp.float32)
    low = norm - high - mid
    extra = jnp.where(lane == 0, high, jnp.where(lane == 1, mid, jnp.where(lane == 2, low, 0.0)))
    table_ref[:, 0:width] = table.astype(jnp.bfloat16)
    table_ref[:, width : 2 * width] = extra.astype(jnp.bfloat16)
    sums_ref[...] = jnp.zeros_like(sums_ref)
    for keys_ref in key_refs:

        def step(at, carry, keys_ref=keys_ref):
            keys = keys_ref[pl.ds(pl.multiple_of(at * tile, tile), tile), :]
            wide = jnp.concatenate([keys, jnp.ones_like(keys)], axis=1)
            scores = lax.dot_general(
                table_ref[...], wide, (((1,), (1,)), ((), ())), preferred_element_type=jnp.float32
            )
            highest = jnp.max(scores, axis=0, keepdims=True)
            spread = jnp.exp2((scores - highest) * rate)
            total = jnp.sum(spread, axis=0, keepdims=True)
            weights = (spread * (1.0 / total)).astype(jnp.bfloat16)
            sums_ref[...] += jnp.dot(weights, wide, preferred_element_type=jnp.float32)
            return carry

        lax.fori_loop(0, keys_ref.shape[0] // tile, step, 0, unroll=2)
    out_ref[0:count] = sums_ref[:, 0:width]
    rows = lax.broadcasted_iota(jnp.int32, (TAIL, width), 0)
    tail = jnp.zeros((TAIL, width), jnp.float32)
    for block in range(count // width):
        mass = jnp.transpose(sums_ref[pl.ds(block * width, width), width : 2 * width])[0:TAIL]
        tail = jnp.where(rows == block, mass, tail)
    out_ref[count : count + TAIL] = tail


def home_sweep(temp, keys, table, tile):
    count, width = table.shape
    vmem = pl.BlockSpec(memory_space=pltpu.VMEM)
    return pl.pallas_call(
        functools.partial(home_sweep_kernel, tile),
        out_shape=jax.ShapeDtypeStruct((count + TAIL, width), jnp.float32),
        in_specs=[pl.BlockSpec(memory_space=pltpu.SMEM)] + [vmem] * (len(keys) + 1),
        out_specs=vmem,
        scratch_shapes=[
            pltpu.VMEM((count, 2 * width), jnp.float32),
            pltpu.VMEM((count, 2 * width), jnp.bfloat16),
        ],
        name="home_sweep",
    )(temp, *keys, table)


def home_renew_kernel(left_ref, right_ref, table_ref, out_ref):
    count, width = table_ref.shape
    mass = left_ref[count : count + TAIL] + right_ref[count : count + TAIL]
    for block in range(count // width):
        rows = slice(block * width, (block + 1) * width)
        spread = jnp.transpose(jnp.broadcast_to(mass[block : block + 1], (width, width)))
        body = left_ref[rows] + right_ref[rows]
        out_ref[rows] = (body + PRIOR * table_ref[rows]) / (spread + PRIOR)


def home_renew(left, right, table):
    return pl.pallas_call(
        home_renew_kernel, out_shape=jax.ShapeDtypeStruct(table.shape, table.dtype), name="home_renew"
    )(left, right, table)


def on_home_chips(key_cache, value_cache, centroids, inv_temp, page_owner):
    heads, tokens, width = key_cache.shape
    pages = tokens // PAGE
    ranks, cores = lax.axis_size("seq"), lax.axis_size("sub")
    me, core = lax.axis_index("seq"), lax.axis_index("sub")
    capacity = max(2, (3 * pages + 2 * ranks - 1) // (2 * ranks))
    half = capacity // cores
    owner = page_owner[:, :, 0]
    paged = (heads, pages, PAGE, width)

    def across(value):
        return lax.ppermute(value, "sub", [(0, 1), (1, 0)])

    def facing(value, bit):
        return lax.ppermute(value, "seq", [(i, i ^ bit) for i in range(ranks)])

    lowered = lower_keys(key_cache.reshape(paged), cores)
    homed = [lowered[0]] + [None] * 3
    for bit in range(1, ranks):
        homed[bit] = facing(lowered[bit], bit)

    owner_after, value_after = tied(owner, value_cache, lowered[1])[:2]
    *value_chunks, moved_values = pack_pages(owner_after, value_after.reshape(paged), VALUE_PLAN, capacity, False)
    values_in = [facing(value_chunks[i], VALUE_PLAN[i][0]) for i in range(len(VALUE_PLAN))]

    owner_after, key_after = tied(owner, key_cache, value_chunks[0])[:2]
    owners = [owner] + [facing(owner_after, bit) for bit in range(1, ranks)]
    *key_chunks, moved_keys = pack_pages(owner_after, key_after.reshape(paged), KEY_PLAN, capacity, True)
    keys_in = [facing(key_chunks[i], KEY_PLAN[i][0]) for i in range(len(KEY_PLAN) - 1)]

    seeds = lax.dynamic_index_in_dim(centroids, me, 0, keepdims=False)
    seeds_got = across(seeds)
    table = jnp.where(
        core == 0, jnp.concatenate([seeds, seeds_got], axis=0), jnp.concatenate([seeds_got, seeds], axis=0)
    )
    keys = [part.reshape(part.shape[0] * PAGE, width) for part in homed]
    for iteration in range(ITERS):
        sums = home_sweep(inv_temp, keys, table, 512)
        if iteration == 0:
            homed_got = [across(homed[bit]) for bit in (1, 2, 3)]
            moved_keys, relayed = home_pages(owners[1:], homed[1:], homed_got, moved_keys, capacity)
            relayed_in = facing(relayed, 1)
        table = home_renew(sums, across(sums), table)
        if iteration == 0:
            table, _ = tied(table, relayed)

    ours = lax.dynamic_slice_in_dim(table, core * (table.shape[0] // cores), table.shape[0] // cores, 0)
    opposite = facing(ours, 2)
    last, _ = tied(key_chunks[-1], table)
    keys_in.append(facing(last, KEY_PLAN[-1][0]))
    near = facing(jnp.stack([ours, opposite]), 1)

    def place(whole, part, head, slot):
        return lax.dynamic_update_slice(whole, part, (head, slot, 0, 0))

    def place_both(whole, part, bit, head):
        part, _ = tied(part, table)
        base = (me ^ bit) * capacity
        other = across(part)
        whole = place(whole, part, head, base + core * half)
        return place(whole, other, head, base + (1 - core) * half)

    for i, (bit, heads_of, _) in enumerate(VALUE_PLAN):
        moved_values = place_both(moved_values, values_in[i], bit, 0)
    for i, (bit, heads_of, _) in enumerate(KEY_PLAN):
        if i == len(KEY_PLAN) - 1:
            relayed_in, _ = tied(relayed_in, table)
            for part, side in ((relayed_in, core), (across(relayed_in), 1 - core)):
                moved_keys = place(moved_keys, part[None], me ^ 1, (me ^ 3 ^ side) * capacity)
        moved_keys = place_both(moved_keys, keys_in[i], bit, heads_of(me ^ bit, bit)[0])

    clusters = jnp.zeros(centroids.shape, centroids.dtype)
    for part, head in ((ours, me), (opposite, me ^ 2), (near[0], me ^ 1), (near[1], me ^ 3)):
        clusters = lax.dynamic_update_slice(clusters, part[None], (head, 0, 0))
    sources = [me ^ bit for bit in range(ranks)]
    return (clusters, moved_keys, moved_values, slot_pages(owners, sources, pages, capacity))


def slot_pages(owners, sources, pages, capacity):
    me = lax.axis_index("seq")
    slot_ids = jnp.arange(capacity, dtype=jnp.int32)
    heads = owners[0].shape[0]
    ids = jnp.full((heads, len(owners) * capacity), -1, jnp.int32)
    for owner, source in zip(owners, sources):
        hits = (owner == me).astype(jnp.int32)
        before = jnp.cumsum(hits, axis=1) - hits
        matched = (hits[:, None, :] == 1) & (before[:, None, :] == slot_ids[None, :, None])
        number = source * pages + jnp.arange(pages, dtype=jnp.int32)
        found = jnp.max(jnp.where(matched, number[None, None, :], -1), axis=2)
        ids = lax.dynamic_update_slice(ids, found, (0, source * capacity))
    return ids


def on_device(key_cache, value_cache, centroids, inv_temp, page_owner):
    heads, tokens, width = key_cache.shape
    pages = tokens // PAGE
    ranks = lax.axis_size("seq")
    cores = lax.axis_size("sub")
    me, core = lax.axis_index("seq"), lax.axis_index("sub")
    share = heads // cores
    capacity = max(2, (3 * pages + 2 * ranks - 1) // (2 * ranks))
    owner = page_owner[:, :, 0]
    swap = [(0, 1), (1, 0)]
    ring = lambda shift: [(i, (i + shift) % ranks) for i in range(ranks)]
    facing = lambda bit: [(i, i ^ bit) for i in range(ranks)]

    owners = [owner] + [lax.ppermute(owner, "seq", ring(shift)) for shift in range(1, ranks)]

    mine = lax.dynamic_slice_in_dim(centroids, core * share, share, 0)
    theirs = lax.dynamic_slice_in_dim(centroids, (1 - core) * share, share, 0)
    got = lax.ppermute(theirs, "sub", swap)
    straight = lax.rem(me, 2) == core
    own = jnp.where(straight, mine, got)
    other = jnp.where(straight, got, mine)

    plan = chunk_plan(ranks, share, capacity)
    *value_chunks, moved_values = scatter_pages(owner, value_cache, plan, ranks, capacity, False)
    *key_chunks, keys_low, moved_keys = scatter_pages(owner, key_cache, plan, ranks, capacity, True)
    keys_low = keys_low.reshape(share, tokens, width)

    waiting = [(0, spec, chunk) for spec, chunk in zip(plan, value_chunks)]
    waiting += [(1, spec, chunk) for spec, chunk in zip(plan, key_chunks)]
    moved = [moved_values, moved_keys]
    arrived = []

    def issue(count, after=None):
        for _ in range(count):
            if not waiting:
                return
            which, spec, chunk = waiting.pop(0)
            if after is not None:
                chunk, _ = tied(chunk, after)
            arrived.append((which, spec, lax.ppermute(chunk, "seq", ring(spec[0]))))

    stages = ITERS * (1 + ranks.bit_length())
    per_stage = -(-len(waiting) // (stages + 1))
    issue(2)
    for _ in range(ITERS):
        keep, send = sweep(inv_temp, keys_low, own, other, 512)
        got = lax.ppermute(send, "seq", facing(1))
        issue(per_stage, send)
        payload = join(keep, got)
        bit = 2
        while bit < ranks:
            got = lax.ppermute(payload, "seq", facing(bit))
            issue(per_stage, payload)
            bit *= 2
            if bit < ranks:
                payload = join(payload, got)
        own = renew(payload, got, own)
        other = lax.ppermute(own, "seq", facing(1))
        issue(per_stage, own)
    issue(len(waiting))

    for which, (shift, head, first, size), chunk in arrived:
        partner = lax.ppermute(chunk, "sub", swap)
        start = lax.rem(me - shift + ranks, ranks) * capacity + first
        place = lambda whole, part, at: lax.dynamic_update_slice(whole, part[None], (at, start, 0, 0))
        moved[which] = place(moved[which], chunk, core * share + head)
        moved[which] = place(moved[which], partner, (1 - core) * share + head)

    lower = jnp.where(lax.rem(me, 2) == 0, own, other)
    upper = jnp.where(lax.rem(me, 2) == 0, other, own)
    ours = jnp.where(core == 0, lower, upper)
    other_half = lax.ppermute(jnp.where(core == 0, upper, lower), "sub", swap)
    clusters = jnp.where(
        core == 0, jnp.concatenate([ours, other_half], axis=0), jnp.concatenate([other_half, ours], axis=0)
    )

    sources = [lax.rem(me - shift + ranks, ranks) for shift in range(ranks)]
    ids = slot_pages(owners, sources, pages, capacity)
    return (clusters, moved[1], moved[0], ids)


def choose(key_cache, value_cache, centroids, inv_temp, page_owner):
    ranks, cores = lax.axis_size("seq"), lax.axis_size("sub")
    homes = ranks == 4 and key_cache.shape[0] == ranks and cores == 2
    if not homes:
        return on_device(key_cache, value_cache, centroids, inv_temp, page_owner)
    return on_home_chips(key_cache, value_cache, centroids, inv_temp, page_owner)


def solution(mesh):
    return jax.shard_map(
        choose,
        mesh=mesh,
        in_specs=(
            P("head", ("rep", "seq"), None),
            P("head", ("rep", "seq"), None),
            P("head", ("rep", "sub"), None),
            P("head"),
            P("head", ("rep", "seq"), None),
        ),
        out_specs=(
            P("head", ("rep", "sub"), None),
            P("head", ("rep", "seq"), None, None),
            P("head", ("rep", "seq"), None, None),
            P("head", ("rep", "seq")),
        ),
        check_vma=False,
    )
```

```python
import functools

import jax
import jax.numpy as jnp
from jax import lax
from jax.experimental import pallas as pl
from jax.experimental.pallas import tpu as pltpu
from jax.sharding import PartitionSpec as P


ITERS = 3
PAGE = 128
PRIOR = 8.0
TAIL = 16
LOG2E = 1.4426950408889634


def chunk_plan(ranks, heads, capacity):
    plan = []
    for head in range(heads):
        for shift in range(1, ranks):
            crossing = min(shift, ranks - shift)
            pieces = crossing if capacity % crossing == 0 else 1
            for piece in range(pieces):
                plan.append((shift, head, piece * (capacity // pieces), capacity // pieces))
    return plan


def fill_table(owner_ref, table_ref, count_ref, head, ranks, capacity, pages):
    def clear(slot, carry):
        table_ref[slot] = pages
        return carry

    lax.fori_loop(0, ranks * capacity, clear, 0)
    for rank in range(ranks):
        count_ref[rank] = 0

    def put(page, carry):
        owner = owner_ref[head, page]
        place = count_ref[owner]
        table_ref[owner * capacity + place] = page
        count_ref[owner] = place + 1
        return carry

    lax.fori_loop(0, pages, put, 0)


def scatter_kernel(plan, ranks, capacity, pages, with_cast, owner_ref, cache_ref, *refs):
    chunk_refs, refs = refs[: len(plan)], refs[len(plan) :]
    if with_cast:
        low_ref, local_ref, wide_ref, page_ref, table_ref, count_ref, in_sem, chunk_sem, local_sem, low_sem = refs
    else:
        local_ref, page_ref, table_ref, count_ref, in_sem, chunk_sem, local_sem = refs
    heads = cache_ref.shape[0]
    me = lax.axis_index("seq")
    core = lax.axis_index("sub")
    share = heads // lax.axis_size("sub")
    order = [(core * share + i) for i in range(share)]
    order += [lax.rem(core * share + i, heads) for i in range(share, heads)]
    into = wide_ref if with_cast else page_ref
    loads = []
    for i, head in enumerate(order):
        target = into.at[i] if with_cast else into.at[i, pl.ds(0, pages)]
        load = pltpu.make_async_copy(cache_ref.at[head], target, in_sem.at[i])
        load.start()
        loads.append(load)
    for i in range(heads):
        page_ref[i, pages] = jnp.zeros(page_ref.shape[2:], page_ref.dtype)
    for i, head in enumerate(order):
        fill_table(owner_ref, table_ref, count_ref, head, ranks, capacity, pages)
        loads[i].wait()
        if with_cast:

            def cast(page, carry, i=i):
                page_ref[i, page] = wide_ref[i, page].astype(page_ref.dtype)
                return carry

            lax.fori_loop(0, pages, cast, 0, unroll=2)
            if i < share:
                pltpu.make_async_copy(page_ref.at[i, pl.ds(0, pages)], low_ref.at[i], low_sem.at[i]).start()
        for j, (shift, chunk_head, first, size) in enumerate(plan):
            if chunk_head != i:
                continue
            base = lax.rem(me + shift, ranks) * capacity + first

            def send(slot, carry, i=i, j=j, base=base):
                page = table_ref[base + slot]
                pltpu.make_async_copy(page_ref.at[i, page], chunk_refs[j].at[slot], chunk_sem.at[j]).start()
                return carry

            lax.fori_loop(0, size, send, 0)

        def keep(slot, carry, i=i, head=head):
            place = me * capacity + slot
            page = table_ref[place]
            pltpu.make_async_copy(page_ref.at[i, page], local_ref.at[head, place], local_sem).start()
            return carry

        lax.fori_loop(0, capacity, keep, 0)
    for j in range(len(plan)):
        pltpu.make_async_copy(chunk_refs[j], chunk_refs[j], chunk_sem.at[j]).wait()
    if with_cast:
        for i in range(share):
            pltpu.make_async_copy(low_ref.at[i], low_ref.at[i], low_sem.at[i]).wait()
    kept = local_ref.at[:, pl.ds(0, capacity)]
    pltpu.make_async_copy(kept, kept, local_sem).wait()


def scatter_pages(owner, cache, plan, ranks, capacity, with_cast):
    heads, tokens, width = cache.shape
    pages = tokens // PAGE
    share = heads // lax.axis_size("sub")
    page_shape = (PAGE, width)
    low = jnp.bfloat16
    anywhere = pl.BlockSpec(memory_space=pl.ANY)
    out_shape = [jax.ShapeDtypeStruct((size,) + page_shape, low) for _, _, _, size in plan]
    if with_cast:
        out_shape.append(jax.ShapeDtypeStruct((share, pages) + page_shape, low))
    out_shape.append(jax.ShapeDtypeStruct((heads, ranks * capacity) + page_shape, low))
    scratch = []
    if with_cast:
        scratch.append(pltpu.VMEM((heads, pages) + page_shape, cache.dtype))
    scratch += [
        pltpu.VMEM((heads, pages + 1) + page_shape, low),
        pltpu.SMEM((ranks * capacity,), jnp.int32),
        pltpu.SMEM((ranks,), jnp.int32),
        pltpu.SemaphoreType.DMA((heads,)),
        pltpu.SemaphoreType.DMA((len(plan),)),
        pltpu.SemaphoreType.DMA,
    ]
    if with_cast:
        scratch.append(pltpu.SemaphoreType.DMA((share,)))
    return pl.pallas_call(
        functools.partial(scatter_kernel, plan, ranks, capacity, pages, with_cast),
        out_shape=out_shape,
        in_specs=[pl.BlockSpec(memory_space=pltpu.SMEM), anywhere],
        out_specs=[anywhere] * len(out_shape),
        scratch_shapes=scratch,
        name="scatter_keys" if with_cast else "scatter_values",
        cost_estimate=pl.CostEstimate(flops=0, bytes_accessed=16 << 20, transcendentals=0),
    )(owner, cache.reshape((heads, pages) + page_shape))


def tail_rows(first, second, dtype):
    rows = lax.broadcasted_iota(jnp.int32, (TAIL, PAGE), 0)
    return jnp.where(rows == 0, first, jnp.where(rows == 1, second, 0.0)).astype(dtype)


def split_mass(mass):
    high = mass.astype(jnp.bfloat16).astype(jnp.float32)
    rows = lax.broadcasted_iota(jnp.int32, mass.shape, 0)
    blocks = mass.shape[0] // 2
    held = jnp.where(rows < blocks // 4, high, 0.0)
    rest = jnp.where(rows < blocks // 4, mass - high, 0.0)
    return (held + pltpu.roll(rest, blocks // 4, 0)).astype(jnp.bfloat16)


def join_mass(tail):
    wide = tail.astype(jnp.float32)
    return wide + pltpu.roll(wide, TAIL - TAIL // 8, 0)


def sweep_kernel(tile, temp_ref, keys_ref, own_ref, other_ref, keep_ref, send_ref, sums_ref, table_ref):
    half, width = own_ref.shape[1:]
    core = lax.axis_index("sub")
    rate = temp_ref[core * pl.num_programs(0) + pl.program_id(0)] * LOG2E
    lane = lax.broadcasted_iota(jnp.int32, (half, width), 1)
    for part, ref in ((0, own_ref), (1, other_ref)):
        table = ref[0]
        norm = -0.5 * jnp.sum(table * table, axis=1, keepdims=True)
        high = norm.astype(jnp.bfloat16).astype(jnp.float32)
        mid = (norm - high).astype(jnp.bfloat16).astype(jnp.float32)
        low = norm - high - mid
        extra = jnp.where(lane == 0, high, jnp.where(lane == 1, mid, jnp.where(lane == 2, low, 0.0)))
        rows = pl.ds(part * half, half)
        table_ref[rows, 0:width] = table.astype(jnp.bfloat16)
        table_ref[rows, width : 2 * width] = extra.astype(jnp.bfloat16)
    sums_ref[...] = jnp.zeros_like(sums_ref)

    def step(at, carry):
        keys = keys_ref[0, pl.ds(pl.multiple_of(at * tile, tile), tile), :]
        wide = jnp.concatenate([keys, jnp.ones_like(keys)], axis=1)
        scores = lax.dot_general(
            table_ref[...], wide, (((1,), (1,)), ((), ())), preferred_element_type=jnp.float32
        )
        highest = jnp.max(scores, axis=0, keepdims=True)
        spread = jnp.exp2((scores - highest) * rate)
        total = jnp.sum(spread, axis=0, keepdims=True)
        weights = (spread * (1.0 / total)).astype(jnp.bfloat16)
        sums_ref[...] += jnp.dot(weights, wide, preferred_element_type=jnp.float32)
        return carry

    lax.fori_loop(0, keys_ref.shape[1] // tile, step, 0, unroll=2)
    masses = []
    for block in range(2 * half // width):
        masses.append(jnp.transpose(sums_ref[pl.ds(block * width, width), width : 2 * width])[0:TAIL])
    keep_ref[0, 0:half] = sums_ref[0:half, 0:width]
    keep_ref[0, half : half + TAIL] = tail_rows(masses[0], masses[1], jnp.float32)
    send_ref[0, 0:half] = sums_ref[half : 2 * half, 0:width].astype(jnp.bfloat16)
    send_ref[0, half : half + TAIL] = split_mass(tail_rows(masses[2], masses[3], jnp.float32))


def sweep(temp, keys, own, other, tile):
    heads, tokens, width = keys.shape
    half = own.shape[1]
    table_spec = pl.BlockSpec((1, half, width), lambda h: (h, 0, 0))
    load_spec = pl.BlockSpec((1, half + TAIL, width), lambda h: (h, 0, 0))
    return pl.pallas_call(
        functools.partial(sweep_kernel, tile),
        grid=(heads,),
        in_specs=[
            pl.BlockSpec(memory_space=pltpu.SMEM),
            pl.BlockSpec((1, tokens, width), lambda h: (h, 0, 0)),
            table_spec,
            table_spec,
        ],
        out_specs=[load_spec, load_spec],
        out_shape=[
            jax.ShapeDtypeStruct((heads, half + TAIL, width), jnp.float32),
            jax.ShapeDtypeStruct((heads, half + TAIL, width), jnp.bfloat16),
        ],
        scratch_shapes=[
            pltpu.VMEM((2 * half, 2 * width), jnp.float32),
            pltpu.VMEM((2 * half, 2 * width), jnp.bfloat16),
        ],
        name="sweep",
        cost_estimate=pl.CostEstimate(
            flops=8 * heads * tokens * half * width, bytes_accessed=2 * heads * tokens * width, transcendentals=2 * heads * tokens * half
        ),
    )(temp, keys, own, other)


def join_kernel(left_ref, right_ref, out_ref):
    half = left_ref.shape[1] - TAIL
    for head in range(left_ref.shape[0]):
        body = left_ref[head, 0:half].astype(jnp.float32) + right_ref[head, 0:half].astype(jnp.float32)
        out_ref[head, 0:half] = body.astype(jnp.bfloat16)
        if left_ref.dtype == jnp.float32:
            mass = left_ref[head, half : half + TAIL]
        else:
            mass = join_mass(left_ref[head, half : half + TAIL])
        mass = mass + join_mass(right_ref[head, half : half + TAIL])
        out_ref[head, half : half + TAIL] = split_mass(mass)


def join(left, right):
    return pl.pallas_call(
        join_kernel,
        out_shape=jax.ShapeDtypeStruct(left.shape, jnp.bfloat16),
        name="join",
    )(left, right)


def renew_kernel(left_ref, right_ref, table_ref, out_ref):
    half, width = table_ref.shape[1:]
    for head in range(left_ref.shape[0]):
        mass = join_mass(left_ref[head, half : half + TAIL]) + join_mass(right_ref[head, half : half + TAIL])
        for block in range(half // width):
            rows = slice(block * width, (block + 1) * width)
            spread = jnp.transpose(jnp.broadcast_to(mass[block : block + 1], (width, width)))
            body = left_ref[head, rows].astype(jnp.float32) + right_ref[head, rows].astype(jnp.float32)
            out_ref[head, rows] = (body + PRIOR * table_ref[head, rows]) / (spread + PRIOR)


def renew(left, right, table):
    return pl.pallas_call(
        renew_kernel,
        out_shape=jax.ShapeDtypeStruct(table.shape, table.dtype),
        name="renew",
    )(left, right, table)


def tied(value, *others):
    return lax.optimization_barrier((value,) + others)


def lower_kernel(cores, cache_ref, *refs):
    ranks = cache_ref.shape[0]
    out_refs, (wide_ref, low_ref, in_sem, out_sem) = refs[:ranks], refs[ranks:]
    part = cache_ref.shape[1] // cores
    first = lax.axis_index("sub") * part
    me = lax.axis_index("seq")
    order = [2, 1, 3, 0]
    for bit in order:
        pltpu.make_async_copy(
            cache_ref.at[me ^ bit, pl.ds(first, part)], wide_ref.at[bit], in_sem.at[bit]
        ).start()
    for bit in order:
        pltpu.make_async_copy(wide_ref.at[bit], wide_ref.at[bit], in_sem.at[bit]).wait()

        def cast(page, carry, bit=bit):
            low_ref[bit, page] = wide_ref[bit, page].astype(low_ref.dtype)
            return carry

        lax.fori_loop(0, part, cast, 0, unroll=2)
        pltpu.make_async_copy(low_ref.at[bit], out_refs[bit], out_sem.at[bit]).start()
    for bit in order:
        pltpu.make_async_copy(low_ref.at[bit], out_refs[bit], out_sem.at[bit]).wait()


def lower_keys(cache, cores):
    ranks, pages = cache.shape[:2]
    part = (pages // cores,) + cache.shape[2:]
    anywhere = pl.BlockSpec(memory_space=pl.ANY)
    return pl.pallas_call(
        functools.partial(lower_kernel, cores),
        out_shape=[jax.ShapeDtypeStruct(part, jnp.bfloat16)] * ranks,
        in_specs=[anywhere],
        out_specs=[anywhere] * ranks,
        scratch_shapes=[
            pltpu.VMEM((ranks,) + part, cache.dtype),
            pltpu.VMEM((ranks,) + part, jnp.bfloat16),
            pltpu.SemaphoreType.DMA((ranks,)),
            pltpu.SemaphoreType.DMA((ranks,)),
        ],
        name="lower_keys",
    )(cache)


def value_heads(me, bit):
    return [0, 1, 2, 3]


def near_pair(me, bit):
    base = ((me ^ 3) >> 1) << 1
    return [base, base + 1]


def near_one(me, bit):
    return [me]


def far_pair(me, bit):
    base = (me >> 1) << 1
    return [base, base + 1]


VALUE_PLAN = ((1, value_heads, 4), (2, value_heads, 4), (3, value_heads, 4))
KEY_PLAN = ((1, near_pair, 2), (1, near_one, 1), (2, far_pair, 2), (3, far_pair, 2))


def pack_kernel(plan, capacity, with_cast, owner_ref, cache_ref, *refs):
    chunk_refs, refs = refs[: len(plan)], refs[len(plan) :]
    if with_cast:
        local_ref, wide_ref, page_ref, table_ref, count_ref, in_sem, chunk_sem, local_sem = refs
    else:
        local_ref, page_ref, table_ref, count_ref, in_sem, chunk_sem, local_sem = refs
    ranks, pages = cache_ref.shape[:2]
    me = lax.axis_index("seq")
    core = lax.axis_index("sub")
    half = capacity // lax.axis_size("sub")
    loads = []
    for head in range(ranks):
        target = wide_ref.at[head] if with_cast else page_ref.at[head, pl.ds(0, pages)]
        load = pltpu.make_async_copy(cache_ref.at[head], target, in_sem.at[head])
        load.start()
        loads.append(load)
    for head in range(ranks):
        page_ref[head, pages] = jnp.zeros(page_ref.shape[2:], page_ref.dtype)
        fill_table(owner_ref, table_ref.at[head], count_ref, head, ranks, capacity, pages)
    for head in range(ranks):
        loads[head].wait()
        if with_cast:

            def cast(page, carry, head=head):
                page_ref[head, page] = wide_ref[head, page].astype(page_ref.dtype)
                return carry

            lax.fori_loop(0, pages, cast, 0, unroll=2)
    for at, (bit, heads_of, _) in enumerate(plan):
        for i, head in enumerate(heads_of(me, bit)):

            def send(slot, carry, at=at, i=i, head=head, bit=bit):
                page = table_ref[head, (me ^ bit) * capacity + core * half + slot]
                pltpu.make_async_copy(page_ref.at[head, page], chunk_refs[at].at[i, slot], chunk_sem.at[at]).start()
                return carry

            lax.fori_loop(0, half, send, 0)
    for head in range(ranks):

        def keep(slot, carry, head=head):
            place = me * capacity + slot
            page = table_ref[head, place]
            pltpu.make_async_copy(page_ref.at[head, page], local_ref.at[head, place], local_sem).start()
            return carry

        lax.fori_loop(0, capacity, keep, 0)
    for at in range(len(plan)):
        pltpu.make_async_copy(chunk_refs[at], chunk_refs[at], chunk_sem.at[at]).wait()
    kept = local_ref.at[:, pl.ds(0, capacity)]
    pltpu.make_async_copy(kept, kept, local_sem).wait()


def pack_pages(owner, cache, plan, capacity, with_cast):
    ranks, pages = cache.shape[:2]
    page_shape = cache.shape[2:]
    half = capacity // lax.axis_size("sub")
    low = jnp.bfloat16
    anywhere = pl.BlockSpec(memory_space=pl.ANY)
    out_shape = [jax.ShapeDtypeStruct((count, half) + page_shape, low) for _, _, count in plan]
    out_shape.append(jax.ShapeDtypeStruct((ranks, ranks * capacity) + page_shape, low))
    scratch = [pltpu.VMEM((ranks, pages) + page_shape, cache.dtype)] if with_cast else []
    scratch += [
        pltpu.VMEM((ranks, pages + 1) + page_shape, low),
        pltpu.SMEM((ranks, ranks * capacity), jnp.int32),
        pltpu.SMEM((ranks,), jnp.int32),
        pltpu.SemaphoreType.DMA((ranks,)),
        pltpu.SemaphoreType.DMA((len(plan),)),
        pltpu.SemaphoreType.DMA,
    ]
    return pl.pallas_call(
        functools.partial(pack_kernel, plan, capacity, with_cast),
        out_shape=out_shape,
        in_specs=[pl.BlockSpec(memory_space=pltpu.SMEM), anywhere],
        out_specs=[anywhere] * len(out_shape),
        scratch_shapes=scratch,
        name="pack_keys" if with_cast else "pack_values",
    )(owner, cache)


def home_kernel(capacity, *refs):
    owner_refs, own_refs, got_refs = refs[0:3], refs[3:6], refs[6:9]
    _, local_ref, next_ref, page_ref, table_ref, in_sem, local_sem, next_sem = refs[9:]
    part = own_refs[0].shape[0]
    pages = part * lax.axis_size("sub")
    me = lax.axis_index("seq")
    core = lax.axis_index("sub")
    for i in range(3):
        pltpu.make_async_copy(own_refs[i], page_ref.at[i, pl.ds(core * part, part)], in_sem.at[i]).start()
        pltpu.make_async_copy(got_refs[i], page_ref.at[i, pl.ds((1 - core) * part, part)], in_sem.at[3 + i]).start()
        page_ref[i, pages] = jnp.zeros(page_ref.shape[2:], page_ref.dtype)

    def clear(slot, carry):
        for row in range(6):
            table_ref[row, slot] = pages
        return carry

    lax.fori_loop(0, capacity, clear, 0)
    for i in range(3):

        def put(page, counts, i=i):
            mine, near = counts
            owner = owner_refs[i][me, page]
            for row, count, wanted in ((i, mine, me), (3 + i, near, me ^ 1)):

                @pl.when(owner == wanted)
                def _(row=row, count=count):
                    table_ref[row, count] = page

            return mine + jnp.where(owner == me, 1, 0), near + jnp.where(owner == (me ^ 1), 1, 0)

        lax.fori_loop(0, pages, put, (jnp.int32(0), jnp.int32(0)))
    for i in range(3):
        whole = page_ref.at[i, pl.ds(0, part)]
        pltpu.make_async_copy(whole, whole, in_sem.at[i]).wait()
        pltpu.make_async_copy(whole, whole, in_sem.at[3 + i]).wait()

    def relay(slot, carry):
        page = table_ref[4 + core, slot]
        pltpu.make_async_copy(page_ref.at[1 + core, page], next_ref.at[slot], next_sem).start()
        return carry

    lax.fori_loop(0, capacity, relay, 0)
    for i in range(3):

        def keep(slot, carry, i=i):
            page = table_ref[i, slot]
            place = (me ^ (i + 1)) * capacity + slot
            pltpu.make_async_copy(page_ref.at[i, page], local_ref.at[me, place], local_sem).start()
            return carry

        lax.fori_loop(0, capacity, keep, 0)
    pltpu.make_async_copy(next_ref, next_ref, next_sem).wait()
    kept = local_ref.at[0, pl.ds(0, 3 * capacity)]
    pltpu.make_async_copy(kept, kept, local_sem).wait()


def home_pages(owners, own, got, local, capacity):
    page_shape = local.shape[2:]
    pages = own[0].shape[0] * lax.axis_size("sub")
    anywhere = pl.BlockSpec(memory_space=pl.ANY)
    return pl.pallas_call(
        functools.partial(home_kernel, capacity),
        out_shape=[
            jax.ShapeDtypeStruct(local.shape, local.dtype),
            jax.ShapeDtypeStruct((capacity,) + page_shape, local.dtype),
        ],
        in_specs=[pl.BlockSpec(memory_space=pltpu.SMEM)] * 3 + [anywhere] * 7,
        out_specs=[anywhere] * 2,
        scratch_shapes=[
            pltpu.VMEM((3, pages + 1) + page_shape, local.dtype),
            pltpu.SMEM((6, capacity), jnp.int32),
            pltpu.SemaphoreType.DMA((6,)),
            pltpu.SemaphoreType.DMA,
            pltpu.SemaphoreType.DMA,
        ],
        input_output_aliases={9: 0},
        name="home_pages",
    )(*owners, *own, *got, local)


def home_sweep_kernel(tile, temp_ref, *refs):
    key_refs, (center_ref, out_ref, sums_ref, table_ref) = refs[:-4], refs[-4:]
    count, width = center_ref.shape
    rate = temp_ref[lax.axis_index("seq")] * LOG2E
    table = center_ref[...]
    lane = lax.broadcasted_iota(jnp.int32, table.shape, 1)
    norm = -0.5 * jnp.sum(table * table, axis=1, keepdims=True)
    high = norm.astype(jnp.bfloat16).astype(jnp.float32)
    mid = (norm - high).astype(jnp.bfloat16).astype(jnp.float32)
    low = norm - high - mid
    extra = jnp.where(lane == 0, high, jnp.where(lane == 1, mid, jnp.where(lane == 2, low, 0.0)))
    table_ref[:, 0:width] = table.astype(jnp.bfloat16)
    table_ref[:, width : 2 * width] = extra.astype(jnp.bfloat16)
    sums_ref[...] = jnp.zeros_like(sums_ref)
    for keys_ref in key_refs:

        def step(at, carry, keys_ref=keys_ref):
            keys = keys_ref[pl.ds(pl.multiple_of(at * tile, tile), tile), :]
            wide = jnp.concatenate([keys, jnp.ones_like(keys)], axis=1)
            scores = lax.dot_general(
                table_ref[...], wide, (((1,), (1,)), ((), ())), preferred_element_type=jnp.float32
            )
            highest = jnp.max(scores, axis=0, keepdims=True)
            spread = jnp.exp2((scores - highest) * rate)
            total = jnp.sum(spread, axis=0, keepdims=True)
            weights = (spread * (1.0 / total)).astype(jnp.bfloat16)
            sums_ref[...] += jnp.dot(weights, wide, preferred_element_type=jnp.float32)
            return carry

        lax.fori_loop(0, keys_ref.shape[0] // tile, step, 0, unroll=2)
    out_ref[0:count] = sums_ref[:, 0:width]
    rows = lax.broadcasted_iota(jnp.int32, (TAIL, width), 0)
    tail = jnp.zeros((TAIL, width), jnp.float32)
    for block in range(count // width):
        mass = jnp.transpose(sums_ref[pl.ds(block * width, width), width : 2 * width])[0:TAIL]
        tail = jnp.where(rows == block, mass, tail)
    out_ref[count : count + TAIL] = tail


def home_sweep(temp, keys, table, tile):
    count, width = table.shape
    vmem = pl.BlockSpec(memory_space=pltpu.VMEM)
    return pl.pallas_call(
        functools.partial(home_sweep_kernel, tile),
        out_shape=jax.ShapeDtypeStruct((count + TAIL, width), jnp.float32),
        in_specs=[pl.BlockSpec(memory_space=pltpu.SMEM)] + [vmem] * (len(keys) + 1),
        out_specs=vmem,
        scratch_shapes=[
            pltpu.VMEM((count, 2 * width), jnp.float32),
            pltpu.VMEM((count, 2 * width), jnp.bfloat16),
        ],
        name="home_sweep",
    )(temp, *keys, table)


def home_renew_kernel(left_ref, right_ref, table_ref, out_ref):
    count, width = table_ref.shape
    mass = left_ref[count : count + TAIL] + right_ref[count : count + TAIL]
    for block in range(count // width):
        rows = slice(block * width, (block + 1) * width)
        spread = jnp.transpose(jnp.broadcast_to(mass[block : block + 1], (width, width)))
        body = left_ref[rows] + right_ref[rows]
        out_ref[rows] = (body + PRIOR * table_ref[rows]) / (spread + PRIOR)


def home_renew(left, right, table):
    return pl.pallas_call(
        home_renew_kernel, out_shape=jax.ShapeDtypeStruct(table.shape, table.dtype), name="home_renew"
    )(left, right, table)


def ids_kernel(capacity, *refs):
    owner_refs, out_ref = refs[:-1], refs[-1]
    heads, pages = owner_refs[0].shape
    me = lax.axis_index("seq")

    def one_head(head, carry):
        def clear(slot, carry):
            out_ref[head, slot] = -1
            return carry

        lax.fori_loop(0, out_ref.shape[1], clear, 0, unroll=4)
        for bit, owner_ref in enumerate(owner_refs):
            source = me ^ bit

            def put(page, count, owner_ref=owner_ref, source=source):
                hit = owner_ref[head, page] == me

                @pl.when(hit)
                def _():
                    out_ref[head, source * capacity + count] = source * pages + page

                return count + jnp.where(hit, 1, 0)

            lax.fori_loop(0, pages, put, jnp.int32(0), unroll=4)
        return carry

    lax.fori_loop(0, heads, one_head, 0)


def home_ids(owners, capacity):
    smem = pl.BlockSpec(memory_space=pltpu.SMEM)
    return pl.pallas_call(
        functools.partial(ids_kernel, capacity),
        out_shape=jax.ShapeDtypeStruct((owners[0].shape[0], len(owners) * capacity), jnp.int32),
        in_specs=[smem] * len(owners),
        out_specs=smem,
        name="home_ids",
    )(*owners)


def on_home_chips(key_cache, value_cache, centroids, inv_temp, page_owner):
    heads, tokens, width = key_cache.shape
    pages = tokens // PAGE
    ranks, cores = lax.axis_size("seq"), lax.axis_size("sub")
    me, core = lax.axis_index("seq"), lax.axis_index("sub")
    capacity = max(2, (3 * pages + 2 * ranks - 1) // (2 * ranks))
    half = capacity // cores
    owner = page_owner[:, :, 0]
    paged = (heads, pages, PAGE, width)

    def across(value):
        return lax.ppermute(value, "sub", [(0, 1), (1, 0)])

    def facing(value, bit):
        return lax.ppermute(value, "seq", [(i, i ^ bit) for i in range(ranks)])

    lowered = lower_keys(key_cache.reshape(paged), cores)
    homed = [lowered[0]] + [None] * 3
    for bit in range(1, ranks):
        homed[bit] = facing(lowered[bit], bit)

    owner_after, value_after = tied(owner, value_cache, lowered[1])[:2]
    owners = [owner] + [facing(owner_after, bit) for bit in range(1, ranks)]
    *value_chunks, moved_values = pack_pages(owner_after, value_after.reshape(paged), VALUE_PLAN, capacity, False)
    values_in = [facing(value_chunks[i], VALUE_PLAN[i][0]) for i in range(len(VALUE_PLAN))]

    owner_after, key_after = tied(owner, key_cache, value_chunks[0])[:2]
    *key_chunks, moved_keys = pack_pages(owner_after, key_after.reshape(paged), KEY_PLAN, capacity, True)
    keys_in = [facing(key_chunks[i], KEY_PLAN[i][0]) for i in range(len(KEY_PLAN) - 1)]

    ids = home_ids(owners, capacity)

    seeds = lax.dynamic_index_in_dim(centroids, me, 0, keepdims=False)
    seeds_got = across(seeds)
    table = jnp.where(
        core == 0, jnp.concatenate([seeds, seeds_got], axis=0), jnp.concatenate([seeds_got, seeds], axis=0)
    )
    keys = [part.reshape(part.shape[0] * PAGE, width) for part in homed]
    for iteration in range(ITERS):
        sums = home_sweep(inv_temp, keys, table, 512)
        if iteration == 0:
            homed_got = [across(homed[bit]) for bit in (1, 2, 3)]
            moved_keys, relayed = home_pages(owners[1:], homed[1:], homed_got, moved_keys, capacity)
            relayed_in = facing(relayed, 1)
        table = home_renew(sums, across(sums), table)
        if iteration == 0:
            table, _ = tied(table, relayed)

    ours = lax.dynamic_slice_in_dim(table, core * (table.shape[0] // cores), table.shape[0] // cores, 0)
    opposite = facing(ours, 2)
    last, _ = tied(key_chunks[-1], table)
    keys_in.append(facing(last, KEY_PLAN[-1][0]))
    near = facing(jnp.stack([ours, opposite]), 1)

    def place(whole, part, head, slot):
        return lax.dynamic_update_slice(whole, part, (head, slot, 0, 0))

    def place_both(whole, part, bit, head):
        part, _ = tied(part, table)
        base = (me ^ bit) * capacity
        other = across(part)
        whole = place(whole, part, head, base + core * half)
        return place(whole, other, head, base + (1 - core) * half)

    for i, (bit, heads_of, _) in enumerate(VALUE_PLAN):
        moved_values = place_both(moved_values, values_in[i], bit, 0)
    for i, (bit, heads_of, _) in enumerate(KEY_PLAN):
        if i == len(KEY_PLAN) - 1:
            relayed_in, _ = tied(relayed_in, table)
            for part, side in ((relayed_in, core), (across(relayed_in), 1 - core)):
                moved_keys = place(moved_keys, part[None], me ^ 1, (me ^ 3 ^ side) * capacity)
        moved_keys = place_both(moved_keys, keys_in[i], bit, heads_of(me ^ bit, bit)[0])

    clusters = jnp.zeros(centroids.shape, centroids.dtype)
    for part, head in ((ours, me), (opposite, me ^ 2), (near[0], me ^ 1), (near[1], me ^ 3)):
        clusters = lax.dynamic_update_slice(clusters, part[None], (head, 0, 0))
    return (clusters, moved_keys, moved_values, ids)


def slot_pages(owners, sources, pages, capacity):
    me = lax.axis_index("seq")
    slot_ids = jnp.arange(capacity, dtype=jnp.int32)
    heads = owners[0].shape[0]
    ids = jnp.full((heads, len(owners) * capacity), -1, jnp.int32)
    for owner, source in zip(owners, sources):
        hits = (owner == me).astype(jnp.int32)
        before = jnp.cumsum(hits, axis=1) - hits
        matched = (hits[:, None, :] == 1) & (before[:, None, :] == slot_ids[None, :, None])
        number = source * pages + jnp.arange(pages, dtype=jnp.int32)
        found = jnp.max(jnp.where(matched, number[None, None, :], -1), axis=2)
        ids = lax.dynamic_update_slice(ids, found, (0, source * capacity))
    return ids


def on_device(key_cache, value_cache, centroids, inv_temp, page_owner):
    heads, tokens, width = key_cache.shape
    pages = tokens // PAGE
    ranks = lax.axis_size("seq")
    cores = lax.axis_size("sub")
    me, core = lax.axis_index("seq"), lax.axis_index("sub")
    share = heads // cores
    capacity = max(2, (3 * pages + 2 * ranks - 1) // (2 * ranks))
    owner = page_owner[:, :, 0]
    swap = [(0, 1), (1, 0)]
    ring = lambda shift: [(i, (i + shift) % ranks) for i in range(ranks)]
    facing = lambda bit: [(i, i ^ bit) for i in range(ranks)]

    owners = [owner] + [lax.ppermute(owner, "seq", ring(shift)) for shift in range(1, ranks)]

    mine = lax.dynamic_slice_in_dim(centroids, core * share, share, 0)
    theirs = lax.dynamic_slice_in_dim(centroids, (1 - core) * share, share, 0)
    got = lax.ppermute(theirs, "sub", swap)
    straight = lax.rem(me, 2) == core
    own = jnp.where(straight, mine, got)
    other = jnp.where(straight, got, mine)

    plan = chunk_plan(ranks, share, capacity)
    *value_chunks, moved_values = scatter_pages(owner, value_cache, plan, ranks, capacity, False)
    *key_chunks, keys_low, moved_keys = scatter_pages(owner, key_cache, plan, ranks, capacity, True)
    keys_low = keys_low.reshape(share, tokens, width)

    waiting = [(0, spec, chunk) for spec, chunk in zip(plan, value_chunks)]
    waiting += [(1, spec, chunk) for spec, chunk in zip(plan, key_chunks)]
    moved = [moved_values, moved_keys]
    arrived = []

    def issue(count, after=None):
        for _ in range(count):
            if not waiting:
                return
            which, spec, chunk = waiting.pop(0)
            if after is not None:
                chunk, _ = tied(chunk, after)
            arrived.append((which, spec, lax.ppermute(chunk, "seq", ring(spec[0]))))

    stages = ITERS * (1 + ranks.bit_length())
    per_stage = -(-len(waiting) // (stages + 1))
    issue(2)
    for _ in range(ITERS):
        keep, send = sweep(inv_temp, keys_low, own, other, 512)
        got = lax.ppermute(send, "seq", facing(1))
        issue(per_stage, send)
        payload = join(keep, got)
        bit = 2
        while bit < ranks:
            got = lax.ppermute(payload, "seq", facing(bit))
            issue(per_stage, payload)
            bit *= 2
            if bit < ranks:
                payload = join(payload, got)
        own = renew(payload, got, own)
        other = lax.ppermute(own, "seq", facing(1))
        issue(per_stage, own)
    issue(len(waiting))

    for which, (shift, head, first, size), chunk in arrived:
        partner = lax.ppermute(chunk, "sub", swap)
        start = lax.rem(me - shift + ranks, ranks) * capacity + first
        place = lambda whole, part, at: lax.dynamic_update_slice(whole, part[None], (at, start, 0, 0))
        moved[which] = place(moved[which], chunk, core * share + head)
        moved[which] = place(moved[which], partner, (1 - core) * share + head)

    lower = jnp.where(lax.rem(me, 2) == 0, own, other)
    upper = jnp.where(lax.rem(me, 2) == 0, other, own)
    ours = jnp.where(core == 0, lower, upper)
    other_half = lax.ppermute(jnp.where(core == 0, upper, lower), "sub", swap)
    clusters = jnp.where(
        core == 0, jnp.concatenate([ours, other_half], axis=0), jnp.concatenate([other_half, ours], axis=0)
    )

    sources = [lax.rem(me - shift + ranks, ranks) for shift in range(ranks)]
    ids = slot_pages(owners, sources, pages, capacity)
    return (clusters, moved[1], moved[0], ids)


def choose(key_cache, value_cache, centroids, inv_temp, page_owner):
    ranks, cores = lax.axis_size("seq"), lax.axis_size("sub")
    homes = ranks == 4 and key_cache.shape[0] == ranks and cores == 2
    if not homes:
        return on_device(key_cache, value_cache, centroids, inv_temp, page_owner)
    return on_home_chips(key_cache, value_cache, centroids, inv_temp, page_owner)


def solution(mesh):
    return jax.shard_map(
        choose,
        mesh=mesh,
        in_specs=(
            P("head", ("rep", "seq"), None),
            P("head", ("rep", "seq"), None),
            P("head", ("rep", "sub"), None),
            P("head"),
            P("head", ("rep", "seq"), None),
        ),
        out_specs=(
            P("head", ("rep", "sub"), None),
            P("head", ("rep", "seq"), None, None),
            P("head", ("rep", "seq"), None, None),
            P("head", ("rep", "seq")),
        ),
        check_vma=False,
    )
```
